32 devices in a mesh: dp: 16 (over z, x, core), seq: 2 (over y).
Axes of the slice: x: 2, y: 2, z: 4, core: 2. Of those that a mesh axis runs over, the one named last changes fastest.
Arguments:
- tokens: bfloat16 [16, 256, 1024], P('dp', 'seq'), may hold values from -6 to 6
- segments: int32 [16, 256], P('dp', 'seq'), may hold values from 0 to 5, never falling along the last dimension, each value on 1 to 85 neighbouring positions
- cotangent: bfloat16 [16, 256, 1024], P('dp', 'seq'), may hold values from -6 to 6
- qkv_weight: bfloat16 [1024, 3, 1024], P('dp', None, 'seq')
- out_weight: bfloat16 [1024, 1024], P('seq', 'dp'), may hold values from -1.5 to 1.5
- in_weight: bfloat16 [1024, 2, 2624], P('dp', None, 'seq'), may hold values from -0.1875 to 0.1875
- down_weight: bfloat16 [2624, 1024], P('seq', 'dp'), may hold values from -0.125 to 0.125
- attn_gain: float32 [1024], P('dp'), may hold values from 0.25 to 1.75
- mlp_gain: float32 [1024], P('dp'), may hold values from 0.25 to 1.75
Outputs:
- layer_out: bfloat16 [16, 256, 1024], P('dp', 'seq')
- tokens_grad: bfloat16 [16, 256, 1024], P('dp', 'seq')
- qkv_grad: float32 [1024, 3, 1024], P('dp', None, 'seq')
- out_grad: float32 [1024, 1024], P('seq', 'dp')
- in_grad: float32 [1024, 2, 2624], P('dp', None, 'seq')
- down_grad: float32 [2624, 1024], P('seq', 'dp')
- attn_gain_grad: float32 [1024], P('dp')
- mlp_gain_grad: float32 [1024], P('dp')
The draws below stay inside these ranges and needn't reach their ends.
Inputs may be any that keep to these rules, and one draw needn't show every extreme that they name: `segments`: along each sequence the numbers never fall; each of the 6 documents has 1 to 85 tokens, and one has exactly 85.
All inputs are finite; a program needn't handle non-finite values.
Results may differ from the reference program's by a relative error of at most 0.034.
Values may be sent and summed in bfloat16 or wider, within the bound.
A program may use at most 128 MiB of HBM per device.

```python
import math
import jax
import jax.numpy as jnp
import numpy as np
from jax import lax

D = 1024
HEADS = 16
FF = 2624
DOCS = 6
HALO = 64
LEN = 256
SEQS = 16


def draw_qkv_weight(key, part):
    return (jax.random.normal(jax.random.fold_in(key, 13), (D, 3 * D), jnp.float32) * D ** (-0.5)).reshape(D, 3, D).astype(jnp.bfloat16)


def with_spikes(values, key, source, target, shards_of, factor):
    def block_of(position):
        return (jnp.arange(values.shape[position]) // (values.shape[position] // shards_of)).reshape((-1,) + (1,) * (values.ndim - 1 - position))

    first = jax.random.permutation(key, shards_of)[block_of(target)]
    far = (block_of(target) + shards_of // 2) % shards_of
    return jnp.where((block_of(source) == first) | (block_of(source) == far), factor * values, values)


def block_scale(rng, dims, split, least, top_value):
    factor_of = 1.0
    for dim, shards_of in split:
        heights = jax.random.uniform(jax.random.fold_in(jax.random.fold_in(rng, 6), dim), (shards_of,), jnp.float32, least / len(split), top_value / len(split))
        factor_of = factor_of * jnp.repeat(jnp.exp(heights), dims[dim] // shards_of).reshape((-1,) + (1,) * (len(dims) - 1 - dim))
    return factor_of


def split_up(amount, total, limit, slope):
    weights = [(1 << 20) // math.isqrt(standing ** slope) + 1 for standing in range(2, amount + 1)]
    rest, counts = total - limit - (amount - 1), [1] * (amount - 1)
    while rest > 0:
        movable = [i for i in range(amount - 1) if counts[i] < limit]
        mass, left = sum([weights[i] for i in movable]), rest
        for i in movable:
            addition = min(limit - counts[i], max(1, left * weights[i] // mass), rest)
            counts[i] = counts[i] + addition
            rest = rest - addition
    return np.array([limit] + counts)


def uneven(stream_key, number_of, total, most, skew):
    if number_of == 2:
        one = jax.random.randint(stream_key, (), max(1, total - most), min(most, total - 1) + 1)
        return jnp.stack([one, total - one])
    tallies = jnp.asarray(split_up(number_of, total, most, skew), jnp.int32)
    twos = (number_of - 1) // 2
    donor, taker = tallies[1:1 + 2 * twos:2], tallies[2:2 + 2 * twos:2]
    slack = jnp.minimum(donor - 1, most - taker)
    moved = jax.random.randint(jax.random.fold_in(stream_key, 1), (twos,), 0, 1 << 20) % (slack + 1)
    tallies = tallies.at[1:1 + 2 * twos:2].set(donor - moved).at[2:2 + 2 * twos:2].set(taker + moved)
    return tallies[jax.random.permutation(jax.random.fold_in(stream_key, 2), number_of)]


def centred(stream_key, shape, deviation, bound, cuts=(), held_as=jnp.bfloat16):
    entries = deviation * jax.random.normal(stream_key, shape, jnp.float32)
    if cuts:
        entries = entries * block_scale(stream_key, shape, cuts, -0.22, 0.18)
    return jnp.clip(entries, -bound, bound).astype(held_as)


def noise_with(key, extent, width, most, pieces, heavy, held_as=jnp.bfloat16):
    result = width * jax.random.normal(key, extent, jnp.float32)
    if pieces:
        result = result * block_scale(key, extent, pieces, -0.22, 0.18)
    return jnp.clip(with_spikes(result, jax.random.fold_in(key, 3), *heavy), -most, most).astype(held_as)


def setup_inputs(seed: int = 0) -> dict:
    key_list = jax.random.split(jax.random.key(seed), 10)
    tokens = noise_with(key_list[0], (SEQS, LEN, D), 1.0, 6.0, ((0, 16), (1, 2)), (1, 2, 2, 2.0))
    segments = jax.vmap(lambda own: jnp.searchsorted(jnp.cumsum(uneven(own, DOCS, LEN, LEN // 3, 1)), jnp.arange(LEN), side="right"))(jax.random.split(key_list[1], SEQS)).reshape((SEQS, LEN)).astype(jnp.int32)
    cotangent = noise_with(key_list[2], (SEQS, LEN, D), 1.0, 6.0, ((0, 16), (1, 2)), (1, 2, 2, 2.0))
    qkv_weight = draw_qkv_weight(jax.random.fold_in(key_list[9], 71), 0)
    out_weight = centred(key_list[4], (D, D), (D // 64) ** -0.5, 1.5, ((0, 2), (1, 16)))
    in_weight = centred(key_list[5], (D, 2, FF), D ** -0.5, 0.1875, ((0, 16), (2, 2)))
    down_weight = centred(key_list[6], (FF, D), FF ** -0.5, 0.125, ((0, 2), (1, 16)))
    attn_gain = jnp.clip(1.0 + 0.15 * jax.random.normal(key_list[7], (D,), jnp.float32), 0.25, 1.75)
    mlp_gain = jnp.clip(1.0 + 0.15 * jax.random.normal(key_list[8], (D,), jnp.float32), 0.25, 1.75)
    return {"tokens": tokens, "segments": segments, "cotangent": cotangent, "qkv_weight": qkv_weight, "out_weight": out_weight, "in_weight": in_weight, "down_weight": down_weight, "attn_gain": attn_gain, "mlp_gain": mlp_gain}


EPS = 1e-05
THETA = 10000.0
NEG_FILL = -1e+30

def norm_forward(values, gain):
    center = values - lax.optimization_barrier(jnp.mean(values, axis=-1, keepdims=True))
    inv_std = lax.rsqrt(lax.optimization_barrier(jnp.mean(center * center, axis=-1, keepdims=True)) + EPS)
    unit_rows = center * inv_std
    return (unit_rows * gain, unit_rows, inv_std)

def norm_backward(grad_rows, gain, unit_rows, inv_std):
    scaled = grad_rows * gain
    inner = scaled - lax.optimization_barrier(jnp.mean(scaled, axis=-1, keepdims=True)) - unit_rows * lax.optimization_barrier(jnp.mean(scaled * unit_rows, axis=-1, keepdims=True))
    return (inner * inv_std, lax.optimization_barrier(jnp.sum(grad_rows * unit_rows, axis=0)))

def gelu_value(inputs):
    return 0.5 * inputs * (1.0 + lax.erf(inputs * 0.7071067811865476))

def gelu_slope(inputs):
    return 0.5 * (1.0 + lax.erf(inputs * 0.7071067811865476)) + inputs * jnp.exp(-0.5 * inputs * inputs) * 0.3989422804014327

def rotary_tables(positions, head_size):
    half_size = head_size // 2
    freqs = jnp.power(THETA, -(2.0 / head_size) * jnp.arange(half_size, dtype=jnp.float32))
    angles = positions.astype(jnp.float32)[:, None] * freqs[None, :]
    return (jnp.cos(angles)[:, None, :], jnp.sin(angles)[:, None, :])

def rotate(values, cos_table, sin_table):
    half_size = values.shape[-1] // 2
    lower_half = values[..., :half_size]
    upper_half = values[..., half_size:]
    return jnp.concatenate([lower_half * cos_table - upper_half * sin_table, upper_half * cos_table + lower_half * sin_table], axis=-1)

def unrotate(grads, cos_table, sin_table):
    half_size = grads.shape[-1] // 2
    lower_half = grads[..., :half_size]
    upper_half = grads[..., half_size:]
    return jnp.concatenate([lower_half * cos_table + upper_half * sin_table, upper_half * cos_table - lower_half * sin_table], axis=-1)

def window_mask(query_pos, key_pos, query_seg, key_seg, halo_width, total_len):
    near = jnp.abs(query_pos[:, None] - key_pos[None, :]) <= halo_width
    inside = (key_pos >= 0) & (key_pos < total_len)
    return near & inside[None, :] & (query_seg[:, None] == key_seg[None, :])

def block_scores(queries, key_slab, allowed, scale):
    scores = jnp.einsum('qhd,khd->hqk', queries.astype(jnp.float32), key_slab.astype(jnp.float32)) * scale
    return jnp.where(allowed[None], scores, NEG_FILL)

def attend_block(queries, key_slab, value_slab, allowed, scale):
    scores = block_scores(queries, key_slab, allowed, scale)
    top_score = lax.optimization_barrier(jnp.max(scores, axis=-1, keepdims=True))
    total = lax.optimization_barrier(jnp.sum(jnp.exp(scores - top_score), axis=-1, keepdims=True))
    logsum = top_score + jnp.log(total)
    probs = jnp.exp(scores - logsum).astype(jnp.bfloat16)
    mixed = jnp.einsum('hqk,khd->qhd', probs.astype(jnp.float32), value_slab.astype(jnp.float32))
    return (mixed, logsum[..., 0])

def attend_back(queries, key_slab, value_slab, allowed, scale, logsum, mixed_b, dmixed_b):
    scores = block_scores(queries, key_slab, allowed, scale)
    probs = jnp.exp(scores - logsum[..., None])
    probs_b = probs.astype(jnp.bfloat16)
    dmixed32 = dmixed_b.astype(jnp.float32)
    dvalues = jnp.einsum('hqk,qhd->khd', probs_b.astype(jnp.float32), dmixed32)
    dprobs = jnp.einsum('qhd,khd->hqk', dmixed32, value_slab.astype(jnp.float32))
    delta = jnp.transpose(lax.optimization_barrier(jnp.sum(dmixed32 * mixed_b.astype(jnp.float32), axis=-1)))
    dscores = (probs * (dprobs - delta[..., None]) * scale).astype(jnp.bfloat16)
    dqueries = jnp.einsum('hqk,khd->qhd', dscores.astype(jnp.float32), key_slab.astype(jnp.float32))
    dkeys = jnp.einsum('hqk,qhd->khd', dscores.astype(jnp.float32), queries.astype(jnp.float32))
    return (dqueries, dkeys, dvalues)

def layer_sequence(seq_tokens, seq_segments, seq_cot, qkv_weight, out_weight, in_weight, down_weight, attn_gain, mlp_gain):
    seq_len = seq_tokens.shape[0]
    model_width = seq_tokens.shape[1]
    head_size = model_width // HEADS
    halo_width = HALO
    block_rows = min(seq_len, 512)
    scale = 1.0 / head_size ** 0.5
    hidden_units = down_weight.shape[0]
    inputs32 = seq_tokens.astype(jnp.float32)
    normed_one, unit_one, inv_one = norm_forward(inputs32, attn_gain)
    normed_one_b = normed_one.astype(jnp.bfloat16)
    projected = jnp.dot(normed_one_b, qkv_weight, preferred_element_type=jnp.float32)
    positions = jnp.arange(seq_len, dtype=jnp.int32)
    cos_table, sin_table = rotary_tables(positions, head_size)
    queries = rotate(projected[:, :model_width].reshape(seq_len, HEADS, head_size), cos_table, sin_table).astype(jnp.bfloat16)
    keys_rot = rotate(projected[:, model_width:2 * model_width].reshape(seq_len, HEADS, head_size), cos_table, sin_table).astype(jnp.bfloat16)
    values_b = projected[:, 2 * model_width:].reshape(seq_len, HEADS, head_size).astype(jnp.bfloat16)
    pad_spec = ((halo_width, halo_width), (0, 0), (0, 0))
    key_pad = jnp.pad(keys_rot, pad_spec)
    value_pad = jnp.pad(values_b, pad_spec)
    seg_pad = jnp.pad(seq_segments, (halo_width, halo_width), constant_values=-1)
    slab_rows = block_rows + 2 * halo_width
    mixed_parts = []
    logsum_parts = []
    masks = []
    for start in range(0, seq_len, block_rows):
        query_pos = start + jnp.arange(block_rows, dtype=jnp.int32)
        key_pos = start - halo_width + jnp.arange(slab_rows, dtype=jnp.int32)
        allowed = window_mask(query_pos, key_pos, seq_segments[start:start + block_rows], seg_pad[start:start + slab_rows], halo_width, seq_len)
        masks.append(allowed)
        mixed_part, logsum_part = attend_block(queries[start:start + block_rows], key_pad[start:start + slab_rows], value_pad[start:start + slab_rows], allowed, scale)
        mixed_parts.append(mixed_part)
        logsum_parts.append(logsum_part)
    mixed_b = jnp.concatenate(mixed_parts, axis=0).astype(jnp.bfloat16)
    mixed_flat = mixed_b.reshape(seq_len, model_width)
    residual = inputs32 + jnp.dot(mixed_flat, out_weight, preferred_element_type=jnp.float32)
    normed_two, unit_two, inv_two = norm_forward(residual, mlp_gain)
    normed_two_b = normed_two.astype(jnp.bfloat16)
    expanded = jnp.dot(normed_two_b, in_weight, preferred_element_type=jnp.float32)
    gate_in = expanded[:, :hidden_units]
    linear_in = expanded[:, hidden_units:]
    activated = gelu_value(gate_in)
    middle_b = (activated * linear_in).astype(jnp.bfloat16)
    layer_out = (residual + jnp.dot(middle_b, down_weight, preferred_element_type=jnp.float32)).astype(jnp.bfloat16)
    down_grad = jnp.dot(middle_b.T, seq_cot, preferred_element_type=jnp.float32)
    dmiddle = jnp.dot(seq_cot, down_weight.T, preferred_element_type=jnp.float32)
    dexpanded_b = jnp.concatenate([dmiddle * linear_in * gelu_slope(gate_in), dmiddle * activated], axis=1).astype(jnp.bfloat16)
    in_grad = jnp.dot(normed_two_b.T, dexpanded_b, preferred_element_type=jnp.float32)
    dnormed_two = jnp.dot(dexpanded_b, in_weight.T, preferred_element_type=jnp.float32)
    dres_norm, mlp_gain_grad = norm_backward(dnormed_two, mlp_gain, unit_two, inv_two)
    dresidual = seq_cot.astype(jnp.float32) + dres_norm
    dresidual_b = dresidual.astype(jnp.bfloat16)
    out_grad = jnp.dot(mixed_flat.T, dresidual_b, preferred_element_type=jnp.float32)
    dmixed_b = jnp.dot(dresidual_b, out_weight.T, preferred_element_type=jnp.float32).astype(jnp.bfloat16).reshape(seq_len, HEADS, head_size)
    dkey_pad = jnp.zeros((seq_len + 2 * halo_width, HEADS, head_size), jnp.float32)
    dvalue_pad = jnp.zeros((seq_len + 2 * halo_width, HEADS, head_size), jnp.float32)
    dquery_parts = []
    for index, start in enumerate(range(0, seq_len, block_rows)):
        dqueries, dkeys, dvalues = attend_back(queries[start:start + block_rows], key_pad[start:start + slab_rows], value_pad[start:start + slab_rows], masks[index], scale, logsum_parts[index], mixed_b[start:start + block_rows], dmixed_b[start:start + block_rows])
        dquery_parts.append(dqueries)
        dkey_pad = dkey_pad.at[start:start + slab_rows].add(dkeys)
        dvalue_pad = dvalue_pad.at[start:start + slab_rows].add(dvalues)
    dquery_all = unrotate(jnp.concatenate(dquery_parts, axis=0), cos_table, sin_table).reshape(seq_len, model_width)
    dkey_all = unrotate(dkey_pad[halo_width:halo_width + seq_len], cos_table, sin_table).reshape(seq_len, model_width)
    dvalue_all = dvalue_pad[halo_width:halo_width + seq_len].reshape(seq_len, model_width)
    dqkv_b = jnp.concatenate([dquery_all, dkey_all, dvalue_all], axis=1).astype(jnp.bfloat16)
    qkv_grad = jnp.dot(normed_one_b.T, dqkv_b, preferred_element_type=jnp.float32)
    dnormed_one = jnp.dot(dqkv_b, qkv_weight.T, preferred_element_type=jnp.float32)
    dinput_norm, attn_gain_grad = norm_backward(dnormed_one, attn_gain, unit_one, inv_one)
    tokens_grad = (dresidual + dinput_norm).astype(jnp.bfloat16)
    return (layer_out, tokens_grad, (qkv_grad, out_grad, in_grad, down_grad, attn_gain_grad, mlp_gain_grad))

def reference(tokens, segments, cotangent, qkv_weight, out_weight, in_weight, down_weight, attn_gain, mlp_gain):
    in_rows = qkv_weight.shape[0]
    qkv_flat = qkv_weight.reshape(in_rows, qkv_weight.shape[1] * qkv_weight.shape[2])
    in_flat = in_weight.reshape(in_rows, in_weight.shape[1] * in_weight.shape[2])
    initial = (jnp.zeros(qkv_flat.shape, jnp.float32), jnp.zeros(out_weight.shape, jnp.float32), jnp.zeros(in_flat.shape, jnp.float32), jnp.zeros(down_weight.shape, jnp.float32), jnp.zeros(attn_gain.shape, jnp.float32), jnp.zeros(mlp_gain.shape, jnp.float32))

    def one_sequence(carry, inputs):
        seq_tokens, seq_segments, seq_cot = inputs
        layer_out, tokens_grad, grads = layer_sequence(seq_tokens, seq_segments, seq_cot, qkv_flat, out_weight, in_flat, down_weight, attn_gain, mlp_gain)
        carry = tuple((total + piece for total, piece in zip(carry, grads)))
        return (carry, (layer_out, tokens_grad))
    totals, (layer_outs, tokens_grads) = lax.scan(one_sequence, initial, (tokens, segments, cotangent))
    return (layer_outs, tokens_grads, totals[0].reshape(qkv_weight.shape), totals[1], totals[2].reshape(in_weight.shape), totals[3], totals[4], totals[5])
```

```python
import functools
import math

import jax
import jax.numpy as jnp
from jax import lax
from jax.experimental import pallas as pl
from jax.experimental.pallas import tpu as pltpu
from jax.sharding import PartitionSpec as P

HEADS = 16
HALO = 64


EPS = 1e-05
THETA = 10000.0
NEG_FILL = -1e30


def norm_forward(values, gain):
    center = values - jnp.mean(values, axis=-1, keepdims=True)
    inv_std = lax.rsqrt(jnp.mean(center * center, axis=-1, keepdims=True) + EPS)
    unit_rows = center * inv_std
    return (unit_rows * gain, unit_rows, inv_std)


def norm_backward(grad_rows, gain, unit_rows, inv_std):
    scaled = grad_rows * gain
    inner = (
        scaled
        - jnp.mean(scaled, axis=-1, keepdims=True)
        - unit_rows * jnp.mean(scaled * unit_rows, axis=-1, keepdims=True)
    )
    return (inner * inv_std, jnp.sum(grad_rows * unit_rows, axis=0))


def gelu_value(inputs):
    return 0.5 * inputs * (1.0 + lax.erf(inputs * 0.7071067811865476))


def gelu_slope(inputs):
    return (
        0.5 * (1.0 + lax.erf(inputs * 0.7071067811865476))
        + inputs * jnp.exp(-0.5 * inputs * inputs) * 0.3989422804014327
    )


def rotary_tables(positions, head_size):
    half_size = head_size // 2
    freqs = jnp.power(THETA, -(2.0 / head_size) * jnp.arange(half_size, dtype=jnp.float32))
    angles = positions.astype(jnp.float32)[:, None] * freqs[None, :]
    return (jnp.cos(angles)[:, None, :], jnp.sin(angles)[:, None, :])


def rotate(values, cos_table, sin_table):
    half_size = values.shape[-1] // 2
    lower_half = values[..., :half_size]
    upper_half = values[..., half_size:]
    return jnp.concatenate(
        [
            lower_half * cos_table - upper_half * sin_table,
            upper_half * cos_table + lower_half * sin_table,
        ],
        axis=-1,
    )


def unrotate(grads, cos_table, sin_table):
    half_size = grads.shape[-1] // 2
    lower_half = grads[..., :half_size]
    upper_half = grads[..., half_size:]
    return jnp.concatenate(
        [
            lower_half * cos_table + upper_half * sin_table,
            upper_half * cos_table - lower_half * sin_table,
        ],
        axis=-1,
    )


def window_mask(query_pos, key_pos, query_seg, key_seg, halo_width, total_len):
    near = jnp.abs(query_pos[:, None] - key_pos[None, :]) <= halo_width
    inside = (key_pos >= 0) & (key_pos < total_len)
    return near & inside[None, :] & (query_seg[:, None] == key_seg[None, :])


def block_scores(queries, key_slab, allowed, scale):
    scores = (
        jnp.einsum("qhd,khd->hqk", queries, key_slab, preferred_element_type=jnp.float32) * scale
    )
    return jnp.where(allowed[None], scores, NEG_FILL)


def attend_block(queries, key_slab, value_slab, allowed, scale):
    scores = block_scores(queries, key_slab, allowed, scale)
    top_score = jnp.max(scores, axis=-1, keepdims=True)
    total = jnp.sum(jnp.exp(scores - top_score), axis=-1, keepdims=True)
    logsum = top_score + jnp.log(total)
    probs = jnp.exp(scores - logsum).astype(jnp.bfloat16)
    mixed = jnp.einsum("hqk,khd->qhd", probs, value_slab, preferred_element_type=jnp.float32)
    return (mixed, logsum[..., 0])


def attend_back(queries, key_slab, value_slab, allowed, scale, logsum, mixed_b, dmixed_b):
    scores = block_scores(queries, key_slab, allowed, scale)
    probs = jnp.exp(scores - logsum[..., None])
    probs_b = probs.astype(jnp.bfloat16)
    dvalues = jnp.einsum("hqk,qhd->khd", probs_b, dmixed_b, preferred_element_type=jnp.float32)
    dprobs = jnp.einsum("qhd,khd->hqk", dmixed_b, value_slab, preferred_element_type=jnp.float32)
    delta = jnp.transpose(
        jnp.sum(dmixed_b.astype(jnp.float32) * mixed_b.astype(jnp.float32), axis=-1)
    )
    dscores = (probs * (dprobs - delta[..., None]) * scale).astype(jnp.bfloat16)
    dqueries = jnp.einsum("hqk,khd->qhd", dscores, key_slab, preferred_element_type=jnp.float32)
    dkeys = jnp.einsum("hqk,qhd->khd", dscores, queries, preferred_element_type=jnp.float32)
    return (dqueries, dkeys, dvalues)


MESH = pl.DeviceIdType.MESH
VMEM_LIMIT = 60 * 1024 * 1024
LANES = 128


def ring_place(count):
    me = lax.axis_index("dp")
    core = me % 2
    chip = me // 2
    row, column = chip // 2, chip % 2
    place = (1 - column) * row + column * (count - 1 - row)
    return (core, place)


def chip_at(place, count):
    side = place // (count // 2)
    return (1 - side) * (2 * place) + side * (2 * (count - 1 - place) + 1)


def neighbours(core, place, count):
    right = chip_at((place + 1) % count, count) * 2 + core
    left = chip_at((place + count - 1) % count, count) * 2 + core
    return (right, left, lax.axis_index("dp") + 1 - 2 * core)


def greet(devices):
    barrier = pltpu.get_barrier_semaphore()
    for device in devices:
        pl.semaphore_signal(barrier, inc=1, device_id={"dp": device}, device_id_type=MESH)
    pl.semaphore_wait(barrier, len(devices))


def gather_kernel(
    count, shard_ref, full_ref, own_sem, send_sem, recv_sem, pair_send, pair_recv
):
    rows = shard_ref.shape[0]
    half = rows // 2
    core, place = ring_place(count)
    right, left, partner = neighbours(core, place, count)
    targets = (right, left)

    def piece(way, step):
        shift = count - step if way == 0 else step
        owner = chip_at((place + shift) % count, count) * 2 + core
        return full_ref.at[pl.ds(pl.multiple_of(owner * rows + way * half, half), half)]

    def hop(way, step):
        ref = piece(way, step)
        return pltpu.make_async_remote_copy(
            src_ref=ref,
            dst_ref=ref,
            send_sem=send_sem.at[way, step],
            recv_sem=recv_sem.at[way, step],
            device_id={"dp": targets[way]},
            device_id_type=MESH,
        )

    def share(way, step):
        ref = piece(way, step)
        return pltpu.make_async_remote_copy(
            src_ref=ref,
            dst_ref=ref,
            send_sem=pair_send.at[way, step],
            recv_sem=pair_recv.at[way, step],
            device_id={"dp": partner},
            device_id_type=MESH,
        )

    me = lax.axis_index("dp")
    own = pltpu.make_async_copy(
        shard_ref, full_ref.at[pl.ds(pl.multiple_of(me * rows, rows), rows)], own_sem
    )
    own.start()
    greet((right, left, partner))
    own.wait()
    for way in range(2):
        hop(way, 0).start()
        share(way, 0).start()

    def step_body(step, carry):
        for way in range(2):
            hop(way, step - 1).wait_recv()
            hop(way, step).start()
            share(way, step).start()
        return carry

    lax.fori_loop(1, count - 1, step_body, 0)
    for way in range(2):
        hop(way, count - 2).wait_recv()
        share(way, count - 1).start()

    def drain_hops(step, carry):
        for way in range(2):
            hop(way, step).wait_send()
        return carry

    def drain_shares(step, carry):
        for way in range(2):
            share(way, step).wait_send()
            share(way, step).wait_recv()
        return carry

    lax.fori_loop(0, count - 1, drain_hops, 0)
    lax.fori_loop(0, count, drain_shares, 0)


def ring_gather(shard, devices):
    count = devices // 2
    rows, columns = shard.shape
    return pl.pallas_call(
        functools.partial(gather_kernel, count),
        out_shape=jax.ShapeDtypeStruct((devices * rows, columns), shard.dtype),
        in_specs=[pl.BlockSpec(memory_space=pltpu.VMEM)],
        out_specs=pl.BlockSpec(memory_space=pltpu.HBM),
        scratch_shapes=[
            pltpu.SemaphoreType.DMA,
            pltpu.SemaphoreType.DMA((2, count - 1)),
            pltpu.SemaphoreType.DMA((2, count - 1)),
            pltpu.SemaphoreType.DMA((2, count)),
            pltpu.SemaphoreType.DMA((2, count)),
        ],
        compiler_params=pltpu.CompilerParams(
            collective_id=0, has_side_effects=True, vmem_limit_bytes=8 * 1024 * 1024
        ),
        name="ring_gather",
    )(shard)


def scatter_kernel(count, streams, *refs):
    grads = refs[:streams]
    outs = refs[streams : 2 * streams]
    pairs = refs[2 * streams : 3 * streams]
    sends = refs[3 * streams : 4 * streams]
    recvs = refs[4 * streams : 5 * streams]
    send_sem, recv_sem, pair_send, pair_recv = refs[5 * streams :]
    rows = outs[0].shape[0]
    half = rows // 2
    core, place = ring_place(count)
    right, left, partner = neighbours(core, place, count)
    targets = (right, left)

    def block(way, step, which):
        shift = 2 * count - 1 - step if way == 0 else 1 + step
        owner = chip_at((place + shift) % count, count) * 2 + which
        return pl.ds(pl.multiple_of(owner * rows + way * half, half), half)

    def share(way, step, stream):
        return pltpu.make_async_remote_copy(
            src_ref=grads[stream].at[block(way, step, 1 - core)],
            dst_ref=pairs[stream].at[way, step],
            send_sem=pair_send.at[stream, way, step],
            recv_sem=pair_recv.at[stream, way, step],
            device_id={"dp": partner},
            device_id_type=MESH,
        )

    def hop(way, step, stream):
        return pltpu.make_async_remote_copy(
            src_ref=sends[stream].at[way, step],
            dst_ref=recvs[stream].at[way, step],
            send_sem=send_sem.at[stream, way, step],
            recv_sem=recv_sem.at[stream, way, step],
            device_id={"dp": targets[way]},
            device_id_type=MESH,
        )

    def pair_sum(way, step, stream):
        share(way, step, stream).wait_recv()
        own = grads[stream][block(way, step, core), :].astype(jnp.float32)
        return own + pairs[stream][way, step].astype(jnp.float32)

    greet((right, left, partner))

    def start_shares(step, carry):
        for stream in range(streams):
            for way in range(2):
                share(way, step, stream).start()
        return carry

    lax.fori_loop(0, count, start_shares, 0)
    for stream in range(streams):
        for way in range(2):
            sends[stream][way, 0] = pair_sum(way, 0, stream).astype(jnp.bfloat16)
            hop(way, 0, stream).start()

    def step_body(step, carry):
        for stream in range(streams):
            for way in range(2):
                total = pair_sum(way, step, stream)
                hop(way, step - 1, stream).wait_recv()
                total = total + recvs[stream][way, step - 1].astype(jnp.float32)
                sends[stream][way, step] = total.astype(jnp.bfloat16)
                hop(way, step, stream).start()
        return carry

    lax.fori_loop(1, count - 1, step_body, 0)
    for stream in range(streams):
        for way in range(2):
            total = pair_sum(way, count - 1, stream)
            hop(way, count - 2, stream).wait_recv()
            total = total + recvs[stream][way, count - 2].astype(jnp.float32)
            outs[stream][way * half : (way + 1) * half, :] = total

    def drain_hops(step, carry):
        for stream in range(streams):
            for way in range(2):
                hop(way, step, stream).wait_send()
        return carry

    def drain_shares(step, carry):
        for stream in range(streams):
            for way in range(2):
                share(way, step, stream).wait_send()
        return carry

    lax.fori_loop(0, count - 1, drain_hops, 0)
    lax.fori_loop(0, count, drain_shares, 0)


def ring_scatter(grads, devices):
    count = devices // 2
    streams = len(grads)
    rows = grads[0].shape[0] // devices
    half = rows // 2
    widths = [grad.shape[1] for grad in grads]
    vmem = pl.BlockSpec(memory_space=pltpu.VMEM)
    return pl.pallas_call(
        functools.partial(scatter_kernel, count, streams),
        out_shape=[jax.ShapeDtypeStruct((rows, width), jnp.float32) for width in widths],
        in_specs=[vmem] * streams,
        out_specs=[vmem] * streams,
        scratch_shapes=[pltpu.VMEM((2, count, half, width), jnp.bfloat16) for width in widths]
        + [pltpu.VMEM((2, count - 1, half, width), jnp.bfloat16) for width in widths] * 2
        + [pltpu.SemaphoreType.DMA((streams, 2, count - 1))] * 2
        + [pltpu.SemaphoreType.DMA((streams, 2, count))] * 2,
        compiler_params=pltpu.CompilerParams(
            collective_id=1, has_side_effects=True, vmem_limit_bytes=VMEM_LIMIT
        ),
        name="ring_scatter",
    )(*grads)


def turn(values, cos_table, sin_table, low_half):
    half = HEAD_HALF
    swapped = jnp.where(
        low_half, pltpu.roll(values, LANES - half, 1), pltpu.roll(values, half, 1)
    )
    return values * cos_table + swapped * sin_table


HEAD_HALF = 32


def lane_masks(rows):
    lane = lax.broadcasted_iota(jnp.int32, (rows, LANES), 1)
    return (lane % (2 * HEAD_HALF) < HEAD_HALF, lane < 2 * HEAD_HALF)


def allowed_pairs(pos_col, pos_row, seg_col, seg_row):
    near = jnp.abs(pos_col[...] - pos_row[...]) <= HALO
    return near & (seg_col[...] == seg_row[...])


def head_probs(queries, keys, allowed, scale):
    scores = (
        lax.dot_general(
            queries, keys, (((1,), (1,)), ((), ())), preferred_element_type=jnp.float32
        )
        * scale
    )
    scores = jnp.where(allowed, scores, NEG_FILL)
    top_score = jnp.max(scores, axis=-1, keepdims=True)
    total = jnp.sum(jnp.exp(scores - top_score), axis=-1, keepdims=True)
    return jnp.exp(scores - (top_score + jnp.log(total)))


def attend_kernel(
    scale, width, proj, cos_ref, sin_ref, pos_col, pos_row, seg_col, seg_row, qkv_out, mixed_out
):
    rows = proj.shape[0]
    low_half, first = lane_masks(rows)
    cos_table, sin_table = cos_ref[...], sin_ref[...]
    allowed = allowed_pairs(pos_col, pos_row, seg_col, seg_row)
    for start in range(0, width, LANES):
        queries = turn(proj[:, start : start + LANES], cos_table, sin_table, low_half)
        keys = turn(
            proj[:, width + start : width + start + LANES], cos_table, sin_table, low_half
        ).astype(jnp.bfloat16)
        values = proj[:, 2 * width + start : 2 * width + start + LANES]
        qkv_out[:, start : start + LANES] = queries.astype(jnp.bfloat16)
        qkv_out[:, width + start : width + start + LANES] = keys
        qkv_out[:, 2 * width + start : 2 * width + start + LANES] = values.astype(jnp.bfloat16)
        mixed = jnp.zeros((rows, LANES), jnp.float32)
        for head in range(2):
            mine = first if head == 0 else ~first
            probs = head_probs(
                jnp.where(mine, queries, 0.0).astype(jnp.bfloat16), keys, allowed, scale
            ).astype(jnp.bfloat16)
            mixed = mixed + jnp.dot(
                probs,
                jnp.where(mine, values, 0.0).astype(jnp.bfloat16),
                preferred_element_type=jnp.float32,
            )
        mixed_out[:, start : start + LANES] = mixed.astype(jnp.bfloat16)


def attend_back_kernel(
    scale,
    width,
    qkv,
    mixed_ref,
    dmixed_ref,
    cos_ref,
    sin_ref,
    pos_col,
    pos_row,
    seg_col,
    seg_row,
    dqkv_out,
):
    rows = qkv.shape[0]
    low_half, first = lane_masks(rows)
    cos_table, sin_table = cos_ref[...], -sin_ref[...]
    allowed = allowed_pairs(pos_col, pos_row, seg_col, seg_row)
    over_rows = (((0,), (0,)), ((), ()))
    over_lanes = (((1,), (1,)), ((), ()))
    for start in range(0, width, LANES):
        queries = qkv[:, start : start + LANES].astype(jnp.float32)
        keys = qkv[:, width + start : width + start + LANES]
        keys32 = keys.astype(jnp.float32)
        values = qkv[:, 2 * width + start : 2 * width + start + LANES]
        dmixed = dmixed_ref[:, start : start + LANES].astype(jnp.float32)
        products = dmixed * mixed_ref[:, start : start + LANES].astype(jnp.float32)
        dquery = jnp.zeros((rows, LANES), jnp.float32)
        dkey = jnp.zeros((rows, LANES), jnp.float32)
        dvalue = jnp.zeros((rows, LANES), jnp.float32)
        for head in range(2):
            mine = first if head == 0 else ~first
            head_queries = jnp.where(mine, queries, 0.0).astype(jnp.bfloat16)
            head_keys = jnp.where(mine, keys32, 0.0).astype(jnp.bfloat16)
            head_dmixed = jnp.where(mine, dmixed, 0.0).astype(jnp.bfloat16)
            delta = jnp.sum(jnp.where(mine, products, 0.0), axis=-1, keepdims=True)
            probs = head_probs(head_queries, keys, allowed, scale)
            dprobs = lax.dot_general(
                head_dmixed, values, over_lanes, preferred_element_type=jnp.float32
            )
            dscores = (probs * (dprobs - delta) * scale).astype(jnp.bfloat16)
            dvalue = dvalue + lax.dot_general(
                probs.astype(jnp.bfloat16),
                head_dmixed,
                over_rows,
                preferred_element_type=jnp.float32,
            )
            dkey = dkey + lax.dot_general(
                dscores, head_queries, over_rows, preferred_element_type=jnp.float32
            )
            dquery = dquery + jnp.dot(dscores, head_keys, preferred_element_type=jnp.float32)
        dquery = turn(dquery, cos_table, sin_table, low_half)
        dkey = turn(dkey, cos_table, sin_table, low_half)
        dqkv_out[:, start : start + LANES] = dquery.astype(jnp.bfloat16)
        dqkv_out[:, width + start : width + start + LANES] = dkey.astype(jnp.bfloat16)
        dqkv_out[:, 2 * width + start : 2 * width + start + LANES] = dvalue.astype(jnp.bfloat16)


def local_call(kernel, name, out_shape, operands, flops):
    vmem = pl.BlockSpec(memory_space=pltpu.VMEM)
    single = not isinstance(out_shape, list)
    return pl.pallas_call(
        kernel,
        out_shape=out_shape,
        in_specs=[vmem] * len(operands),
        out_specs=vmem if single else [vmem] * len(out_shape),
        cost_estimate=pl.CostEstimate(
            flops=flops, bytes_accessed=4 * 1024 * 1024, transcendentals=flops // 256
        ),
        compiler_params=pltpu.CompilerParams(vmem_limit_bytes=32 * 1024 * 1024),
        name=name,
    )(*operands)


class PairedAttention:
    def __init__(self, positions, segments, head_size, width):
        rows = positions.shape[0]
        cos_table, sin_table = rotary_tables(positions, head_size)
        cos_table, sin_table = cos_table[:, 0, :], sin_table[:, 0, :]
        self.width = width
        self.scale = 1.0 / math.sqrt(head_size)
        self.flops = 2 * rows * rows * LANES * (width // head_size)
        self.shared = (
            jnp.concatenate([cos_table] * 4, axis=1),
            jnp.concatenate([-sin_table, sin_table] * 2, axis=1),
            positions[:, None],
            positions[None, :],
            segments[:, None],
            segments[None, :],
        )

    def forward(self, projected):
        rows = projected.shape[0]
        self.qkv, self.mixed = local_call(
            functools.partial(attend_kernel, self.scale, self.width),
            "attend",
            [
                jax.ShapeDtypeStruct((rows, 3 * self.width), jnp.bfloat16),
                jax.ShapeDtypeStruct((rows, self.width), jnp.bfloat16),
            ],
            (projected,) + self.shared,
            2 * self.flops,
        )
        return self.mixed

    def backward(self, dmixed):
        rows = dmixed.shape[0]
        return local_call(
            functools.partial(attend_back_kernel, self.scale, self.width),
            "attend_back",
            jax.ShapeDtypeStruct((rows, 3 * self.width), jnp.bfloat16),
            (self.qkv, self.mixed, dmixed) + self.shared,
            5 * self.flops,
        )


class BlockAttention:
    def __init__(self, positions, segments, head_size, width):
        self.total_len = positions.shape[0]
        self.segments = segments
        self.head_size = head_size
        self.width = width
        self.scale = 1.0 / math.sqrt(head_size)
        self.cos_table, self.sin_table = rotary_tables(positions, head_size)

    def heads(self, values):
        return values.reshape(self.total_len, self.width // self.head_size, self.head_size)

    def forward(self, projected):
        width, total_len = self.width, self.total_len
        self.block_rows = min(total_len, 512)
        self.slab_rows = self.block_rows + 2 * HALO
        tables = (self.cos_table, self.sin_table)
        self.queries = rotate(self.heads(projected[:, :width]), *tables).astype(jnp.bfloat16)
        keys = rotate(self.heads(projected[:, width : 2 * width]), *tables).astype(jnp.bfloat16)
        values = self.heads(projected[:, 2 * width :]).astype(jnp.bfloat16)
        pad_spec = ((HALO, HALO), (0, 0), (0, 0))
        self.key_pad = jnp.pad(keys, pad_spec)
        self.value_pad = jnp.pad(values, pad_spec)
        seg_pad = jnp.pad(self.segments, (HALO, HALO), constant_values=-1)
        mixed_parts = []
        self.logsums = []
        self.masks = []
        for start in range(0, total_len, self.block_rows):
            own = slice(start, start + self.block_rows)
            slab = slice(start, start + self.slab_rows)
            allowed = window_mask(
                start + jnp.arange(self.block_rows, dtype=jnp.int32),
                start - HALO + jnp.arange(self.slab_rows, dtype=jnp.int32),
                self.segments[own],
                seg_pad[slab],
                HALO,
                total_len,
            )
            mixed, logsum = attend_block(
                self.queries[own], self.key_pad[slab], self.value_pad[slab], allowed, self.scale
            )
            self.masks.append(allowed)
            self.logsums.append(logsum)
            mixed_parts.append(mixed)
        self.mixed = jnp.concatenate(mixed_parts, axis=0).astype(jnp.bfloat16)
        return self.mixed.reshape(total_len, width)

    def backward(self, dmixed):
        total_len = self.total_len
        dmixed = self.heads(dmixed)
        padded = (total_len + 2 * HALO,) + dmixed.shape[1:]
        dkey_pad = jnp.zeros(padded, jnp.float32)
        dvalue_pad = jnp.zeros(padded, jnp.float32)
        dquery_parts = []
        for index, start in enumerate(range(0, total_len, self.block_rows)):
            own = slice(start, start + self.block_rows)
            slab = slice(start, start + self.slab_rows)
            dqueries, dkeys, dvalues = attend_back(
                self.queries[own],
                self.key_pad[slab],
                self.value_pad[slab],
                self.masks[index],
                self.scale,
                self.logsums[index],
                self.mixed[own],
                dmixed[own],
            )
            dquery_parts.append(dqueries)
            dkey_pad = dkey_pad.at[slab].add(dkeys)
            dvalue_pad = dvalue_pad.at[slab].add(dvalues)
        inner = slice(HALO, HALO + total_len)
        tables = (self.cos_table, self.sin_table)
        parts = [
            unrotate(jnp.concatenate(dquery_parts, axis=0), *tables),
            unrotate(dkey_pad[inner], *tables),
            dvalue_pad[inner],
        ]
        return jnp.concatenate(
            [part.reshape(total_len, self.width) for part in parts], axis=1
        ).astype(jnp.bfloat16)


def dot(left, right, left_dim, right_dim):
    return lax.dot_general(
        left,
        right,
        (((left_dim,), (right_dim,)), ((), ())),
        preferred_element_type=jnp.float32,
    )


def padded_to_lanes(values):
    return jnp.pad(values, ((0, 0), (0, -values.shape[1] % LANES)))


def high_and_low(gain):
    high = gain.astype(jnp.bfloat16)
    return [high[:, None], (gain - high.astype(jnp.float32)).astype(jnp.bfloat16)[:, None]]


def per_device(
    devices,
    seq_size,
    tokens,
    segments,
    cotangent,
    qkv_weight,
    out_weight,
    in_weight,
    down_weight,
    attn_gain,
    mlp_gain,
):
    layer_in = tokens[0]
    seg_local = segments[0]
    cot_local = cotangent[0]
    own_rows, model_width = layer_in.shape
    head_size = model_width // HEADS
    local_width = qkv_weight.shape[2]
    local_hidden = in_weight.shape[2]
    shard_rows = qkv_weight.shape[0]
    total_len = own_rows * seq_size
    paired = (
        seq_size == 2
        and total_len <= 512
        and local_width % LANES == 0
        and head_size == 2 * HEAD_HALF
    )
    swap = [(0, 1), (1, 0)]

    def rows_of_all(values):
        if paired:
            return jnp.concatenate([values, lax.ppermute(values, "seq", swap)], axis=0)
        return lax.all_gather(values, "seq", axis=0, tiled=True)

    def sum_to_owner(partial):
        if paired:
            other = lax.ppermute(partial[own_rows:].astype(jnp.bfloat16), "seq", swap)
            return partial[:own_rows] + other.astype(jnp.float32)
        return lax.psum_scatter(
            partial.astype(jnp.bfloat16), "seq", scatter_dimension=0, tiled=True
        ).astype(jnp.float32)

    def sum_over_seq(part):
        if paired:
            return part + lax.ppermute(part, "seq", swap)
        return lax.psum(part, "seq")

    first_pack = jnp.concatenate(
        [qkv_weight.reshape(shard_rows, 3 * local_width), out_weight.T]
        + [
            padded_to_lanes(
                jnp.concatenate(high_and_low(attn_gain) + high_and_low(mlp_gain), axis=1)
            )
        ],
        axis=1,
    )
    second_pack = jnp.concatenate(
        [
            padded_to_lanes(in_weight[:, 0, :]),
            padded_to_lanes(in_weight[:, 1, :]),
            padded_to_lanes(down_weight.T),
        ],
        axis=1,
    )
    wide = second_pack.shape[1] // 3
    first_full = ring_gather(first_pack, devices)
    second_full = lax.all_gather(second_pack, "dp", axis=0, tiled=True)
    full_qkv = first_full[:, : 3 * local_width]
    full_out = first_full[:, 3 * local_width : 4 * local_width]
    gains = first_full[:, 4 * local_width : 4 * local_width + 4].astype(jnp.float32)
    gain_attn = gains[:, 0] + gains[:, 1]
    gain_mlp = gains[:, 2] + gains[:, 3]
    full_in = second_full[:, : 2 * wide]
    full_down = second_full[:, 2 * wide :]

    inputs32 = layer_in.astype(jnp.float32)
    normed_one, unit_one, inv_one = norm_forward(inputs32, gain_attn)
    normed_full = rows_of_all(normed_one.astype(jnp.bfloat16))
    cot_full = rows_of_all(cot_local)
    if paired:
        seg_full = rows_of_all(
            jnp.broadcast_to(seg_local.astype(jnp.float32)[:, None], (own_rows, LANES))
        )[:, 0].astype(jnp.int32)
        place = lax.axis_index("seq")
        arange = jnp.arange(own_rows, dtype=jnp.int32)
        positions = jnp.concatenate(
            [place * own_rows + arange, (1 - place) * own_rows + arange], axis=0
        )
        attention = PairedAttention(positions, seg_full, head_size, local_width)
    else:
        seg_full = rows_of_all(seg_local.astype(jnp.bfloat16)).astype(jnp.int32)
        positions = jnp.arange(total_len, dtype=jnp.int32)
        attention = BlockAttention(positions, seg_full, head_size, local_width)

    mixed = attention.forward(dot(normed_full, full_qkv, 1, 0))
    residual = inputs32 + sum_to_owner(dot(mixed, full_out, 1, 1))
    normed_two, unit_two, inv_two = norm_forward(residual, gain_mlp)
    normed_two_full = rows_of_all(normed_two.astype(jnp.bfloat16))
    expanded = dot(normed_two_full, full_in, 1, 0)
    gate_in = expanded[:, :wide]
    linear_in = expanded[:, wide:]
    activated = gelu_value(gate_in)
    middle_b = (activated * linear_in).astype(jnp.bfloat16)
    layer_out = (residual + sum_to_owner(dot(middle_b, full_down, 1, 1))).astype(jnp.bfloat16)

    down_grad = dot(cot_full, middle_b, 0, 0).astype(jnp.bfloat16)
    down_share = lax.psum_scatter(down_grad, "dp", scatter_dimension=0, tiled=True)
    dmiddle = dot(cot_full, full_down, 1, 0)
    dexpanded_b = jnp.concatenate(
        [dmiddle * linear_in * gelu_slope(gate_in), dmiddle * activated], axis=1
    ).astype(jnp.bfloat16)
    dnormed_two = sum_to_owner(dot(dexpanded_b, full_in, 1, 1))
    in_grad = dot(normed_two_full, dexpanded_b, 0, 0).astype(jnp.bfloat16)
    dres_norm, mlp_gain_part = norm_backward(dnormed_two, gain_mlp, unit_two, inv_two)
    dresidual = cot_local.astype(jnp.float32) + dres_norm
    dres_full = rows_of_all(dresidual.astype(jnp.bfloat16))
    dmixed = dot(dres_full, full_out, 1, 0).astype(jnp.bfloat16)
    out_grad = dot(dres_full, mixed, 0, 0).astype(jnp.bfloat16)
    dqkv_b = attention.backward(dmixed)
    dnormed_one = sum_to_owner(dot(dqkv_b, full_qkv, 1, 1))
    qkv_grad = dot(normed_full, dqkv_b, 0, 0).astype(jnp.bfloat16)
    dinput_norm, attn_gain_part = norm_backward(dnormed_one, gain_attn, unit_one, inv_one)
    tokens_grad = (dresidual + dinput_norm).astype(jnp.bfloat16)
    gain_sums = sum_over_seq(jnp.stack([attn_gain_part, mlp_gain_part]))
    gain_grad = padded_to_lanes(gain_sums.T).astype(jnp.bfloat16)

    in_share, qkv_share, out_share, gain_share = ring_scatter(
        [in_grad, qkv_grad, out_grad, gain_grad], devices
    )
    return (
        layer_out[None],
        tokens_grad[None],
        qkv_share.reshape(shard_rows, 3, local_width),
        out_share.T,
        jnp.stack([in_share[:, :local_hidden], in_share[:, wide : wide + local_hidden]], axis=1),
        down_share.astype(jnp.float32)[:, :local_hidden].T,
        gain_share[:, 0],
        gain_share[:, 1],
    )


def solution(mesh):
    return jax.shard_map(
        functools.partial(per_device, mesh.shape["dp"], mesh.shape["seq"]),
        mesh=mesh,
        in_specs=(
            P("dp", "seq", None),
            P("dp", "seq"),
            P("dp", "seq", None),
            P("dp", None, "seq"),
            P("seq", "dp"),
            P("dp", None, "seq"),
            P("seq", "dp"),
            P("dp"),
            P("dp"),
        ),
        out_specs=(
            P("dp", "seq", None),
            P("dp", "seq", None),
            P("dp", None, "seq"),
            P("seq", "dp"),
            P("dp", None, "seq"),
            P("seq", "dp"),
            P("dp"),
            P("dp"),
        ),
        check_vma=False,
    )
```

```python
import functools
import math

import jax
import jax.numpy as jnp
from jax import lax
from jax.experimental import pallas as pl
from jax.experimental.pallas import tpu as pltpu
from jax.sharding import PartitionSpec as P

HEADS = 16
HALO = 64


EPS = 1e-05
THETA = 10000.0
NEG_FILL = -1e30


def norm_forward(values, gain):
    center = values - jnp.mean(values, axis=-1, keepdims=True)
    inv_std = lax.rsqrt(jnp.mean(center * center, axis=-1, keepdims=True) + EPS)
    unit_rows = center * inv_std
    return (unit_rows * gain, unit_rows, inv_std)


def norm_backward(grad_rows, gain, unit_rows, inv_std):
    scaled = grad_rows * gain
    inner = (
        scaled
        - jnp.mean(scaled, axis=-1, keepdims=True)
        - unit_rows * jnp.mean(scaled * unit_rows, axis=-1, keepdims=True)
    )
    return (inner * inv_std, jnp.sum(grad_rows * unit_rows, axis=0))


def gelu_value(inputs):
    return 0.5 * inputs * (1.0 + lax.erf(inputs * 0.7071067811865476))


def gelu_slope(inputs):
    return (
        0.5 * (1.0 + lax.erf(inputs * 0.7071067811865476))
        + inputs * jnp.exp(-0.5 * inputs * inputs) * 0.3989422804014327
    )


def rotary_tables(positions, head_size):
    half_size = head_size // 2
    freqs = jnp.power(THETA, -(2.0 / head_size) * jnp.arange(half_size, dtype=jnp.float32))
    angles = positions.astype(jnp.float32)[:, None] * freqs[None, :]
    return (jnp.cos(angles)[:, None, :], jnp.sin(angles)[:, None, :])


def rotate(values, cos_table, sin_table):
    half_size = values.shape[-1] // 2
    lower_half = values[..., :half_size]
    upper_half = values[..., half_size:]
    return jnp.concatenate(
        [
            lower_half * cos_table - upper_half * sin_table,
            upper_half * cos_table + lower_half * sin_table,
        ],
        axis=-1,
    )


def unrotate(grads, cos_table, sin_table):
    half_size = grads.shape[-1] // 2
    lower_half = grads[..., :half_size]
    upper_half = grads[..., half_size:]
    return jnp.concatenate(
        [
            lower_half * cos_table + upper_half * sin_table,
            upper_half * cos_table - lower_half * sin_table,
        ],
        axis=-1,
    )


def window_mask(query_pos, key_pos, query_seg, key_seg, halo_width, total_len):
    near = jnp.abs(query_pos[:, None] - key_pos[None, :]) <= halo_width
    inside = (key_pos >= 0) & (key_pos < total_len)
    return near & inside[None, :] & (query_seg[:, None] == key_seg[None, :])


def block_scores(queries, key_slab, allowed, scale):
    scores = (
        jnp.einsum("qhd,khd->hqk", queries, key_slab, preferred_element_type=jnp.float32) * scale
    )
    return jnp.where(allowed[None], scores, NEG_FILL)


def attend_block(queries, key_slab, value_slab, allowed, scale):
    scores = block_scores(queries, key_slab, allowed, scale)
    top_score = jnp.max(scores, axis=-1, keepdims=True)
    total = jnp.sum(jnp.exp(scores - top_score), axis=-1, keepdims=True)
    logsum = top_score + jnp.log(total)
    probs = jnp.exp(scores - logsum).astype(jnp.bfloat16)
    mixed = jnp.einsum("hqk,khd->qhd", probs, value_slab, preferred_element_type=jnp.float32)
    return (mixed, logsum[..., 0])


def attend_back(queries, key_slab, value_slab, allowed, scale, logsum, mixed_b, dmixed_b):
    scores = block_scores(queries, key_slab, allowed, scale)
    probs = jnp.exp(scores - logsum[..., None])
    probs_b = probs.astype(jnp.bfloat16)
    dvalues = jnp.einsum("hqk,qhd->khd", probs_b, dmixed_b, preferred_element_type=jnp.float32)
    dprobs = jnp.einsum("qhd,khd->hqk", dmixed_b, value_slab, preferred_element_type=jnp.float32)
    delta = jnp.transpose(
        jnp.sum(dmixed_b.astype(jnp.float32) * mixed_b.astype(jnp.float32), axis=-1)
    )
    dscores = (probs * (dprobs - delta[..., None]) * scale).astype(jnp.bfloat16)
    dqueries = jnp.einsum("hqk,khd->qhd", dscores, key_slab, preferred_element_type=jnp.float32)
    dkeys = jnp.einsum("hqk,qhd->khd", dscores, queries, preferred_element_type=jnp.float32)
    return (dqueries, dkeys, dvalues)


MESH = pl.DeviceIdType.MESH
VMEM_LIMIT = 60 * 1024 * 1024
LANES = 128


def ring_place(count):
    me = lax.axis_index("dp")
    core = me % 2
    chip = me // 2
    row, column = chip // 2, chip % 2
    place = (1 - column) * row + column * (count - 1 - row)
    return (core, place)


def chip_at(place, count):
    side = place // (count // 2)
    return (1 - side) * (2 * place) + side * (2 * (count - 1 - place) + 1)


def neighbours(core, place, count):
    right = chip_at((place + 1) % count, count) * 2 + core
    left = chip_at((place + count - 1) % count, count) * 2 + core
    return (right, left, lax.axis_index("dp") + 1 - 2 * core)


def greet(devices):
    barrier = pltpu.get_barrier_semaphore()
    for device in devices:
        pl.semaphore_signal(barrier, inc=1, device_id={"dp": device}, device_id_type=MESH)
    pl.semaphore_wait(barrier, len(devices))


def gather_kernel(count, streams, *refs):
    shards = refs[:streams]
    fulls = refs[streams : 2 * streams]
    own_sem, send_sem, recv_sem, pair_send, pair_recv = refs[2 * streams :]
    rows = shards[0].shape[0]
    half = rows // 2
    core, place = ring_place(count)
    right, left, partner = neighbours(core, place, count)
    targets = (right, left)
    lanes = [(way, stream) for stream in range(streams) for way in range(2)]

    def piece(way, step, stream):
        shift = count - step if way == 0 else step
        owner = chip_at((place + shift) % count, count) * 2 + core
        start = pl.multiple_of(owner * rows + way * half, half)
        return fulls[stream].at[pl.ds(start, half)]

    def hop(way, step, stream):
        ref = piece(way, step, stream)
        return pltpu.make_async_remote_copy(
            src_ref=ref,
            dst_ref=ref,
            send_sem=send_sem.at[stream, way, step],
            recv_sem=recv_sem.at[stream, way, step],
            device_id={"dp": targets[way]},
            device_id_type=MESH,
        )

    def share(way, step, stream):
        ref = piece(way, step, stream)
        return pltpu.make_async_remote_copy(
            src_ref=ref,
            dst_ref=ref,
            send_sem=pair_send.at[stream, way, step],
            recv_sem=pair_recv.at[stream, way, step],
            device_id={"dp": partner},
            device_id_type=MESH,
        )

    me = lax.axis_index("dp")
    owns = [
        pltpu.make_async_copy(
            shards[stream],
            fulls[stream].at[pl.ds(pl.multiple_of(me * rows, rows), rows)],
            own_sem.at[stream],
        )
        for stream in range(streams)
    ]
    for own in owns:
        own.start()
    greet((right, left, partner))
    for own in owns:
        own.wait()
    for way, stream in lanes:
        hop(way, 0, stream).start()
        share(way, 0, stream).start()

    def step_body(step, carry):
        for way, stream in lanes:
            hop(way, step - 1, stream).wait_recv()
            hop(way, step, stream).start()
            share(way, step, stream).start()
        return carry

    lax.fori_loop(1, count - 1, step_body, 0)
    for way, stream in lanes:
        hop(way, count - 2, stream).wait_recv()
        share(way, count - 1, stream).start()

    def drain_hops(step, carry):
        for way, stream in lanes:
            hop(way, step, stream).wait_send()
        return carry

    def drain_shares(step, carry):
        for way, stream in lanes:
            share(way, step, stream).wait_send()
            share(way, step, stream).wait_recv()
        return carry

    lax.fori_loop(0, count - 1, drain_hops, 0)
    lax.fori_loop(0, count, drain_shares, 0)


def ring_gather(shards, devices):
    count = devices // 2
    streams = len(shards)
    return pl.pallas_call(
        functools.partial(gather_kernel, count, streams),
        out_shape=[
            jax.ShapeDtypeStruct((devices * shard.shape[0], shard.shape[1]), shard.dtype)
            for shard in shards
        ],
        in_specs=[pl.BlockSpec(memory_space=pltpu.VMEM)] * streams,
        out_specs=[pl.BlockSpec(memory_space=pl.ANY)] * streams,
        scratch_shapes=[pltpu.SemaphoreType.DMA((streams,))]
        + [pltpu.SemaphoreType.DMA((streams, 2, count - 1))] * 2
        + [pltpu.SemaphoreType.DMA((streams, 2, count))] * 2,
        cost_estimate=pl.CostEstimate(
            flops=0, bytes_accessed=128 * 1024 * 1024, transcendentals=0
        ),
        compiler_params=pltpu.CompilerParams(
            collective_id=0, has_side_effects=True, vmem_limit_bytes=VMEM_LIMIT
        ),
        name="ring_gather",
    )(*shards)


def scatter_kernel(count, streams, *refs):
    grads = refs[:streams]
    outs = refs[streams : 2 * streams]
    pairs = refs[2 * streams : 3 * streams]
    sends = refs[3 * streams : 4 * streams]
    recvs = refs[4 * streams : 5 * streams]
    send_sem, recv_sem, pair_send, pair_recv = refs[5 * streams :]
    rows = outs[0].shape[0]
    half = rows // 2
    core, place = ring_place(count)
    right, left, partner = neighbours(core, place, count)
    targets = (right, left)

    def block(way, step, which):
        shift = 2 * count - 1 - step if way == 0 else 1 + step
        owner = chip_at((place + shift) % count, count) * 2 + which
        return pl.ds(pl.multiple_of(owner * rows + way * half, half), half)

    def share(way, step, stream):
        return pltpu.make_async_remote_copy(
            src_ref=grads[stream].at[block(way, step, 1 - core)],
            dst_ref=pairs[stream].at[way, step],
            send_sem=pair_send.at[stream, way, step],
            recv_sem=pair_recv.at[stream, way, step],
            device_id={"dp": partner},
            device_id_type=MESH,
        )

    def hop(way, step, stream):
        return pltpu.make_async_remote_copy(
            src_ref=sends[stream].at[way, step],
            dst_ref=recvs[stream].at[way, step],
            send_sem=send_sem.at[stream, way, step],
            recv_sem=recv_sem.at[stream, way, step],
            device_id={"dp": targets[way]},
            device_id_type=MESH,
        )

    def pair_sum(way, step, stream):
        share(way, step, stream).wait_recv()
        own = grads[stream][block(way, step, core), :].astype(jnp.float32)
        return own + pairs[stream][way, step].astype(jnp.float32)

    greet((right, left, partner))

    def start_shares(step, carry):
        for stream in range(streams):
            for way in range(2):
                share(way, step, stream).start()
        return carry

    lax.fori_loop(0, count, start_shares, 0)
    for stream in range(streams):
        for way in range(2):
            sends[stream][way, 0] = pair_sum(way, 0, stream).astype(jnp.bfloat16)
            hop(way, 0, stream).start()

    def step_body(step, carry):
        for stream in range(streams):
            for way in range(2):
                total = pair_sum(way, step, stream)
                hop(way, step - 1, stream).wait_recv()
                total = total + recvs[stream][way, step - 1].astype(jnp.float32)
                sends[stream][way, step] = total.astype(jnp.bfloat16)
                hop(way, step, stream).start()
        return carry

    lax.fori_loop(1, count - 1, step_body, 0)
    for stream in range(streams):
        for way in range(2):
            total = pair_sum(way, count - 1, stream)
            hop(way, count - 2, stream).wait_recv()
            total = total + recvs[stream][way, count - 2].astype(jnp.float32)
            outs[stream][way * half : (way + 1) * half, :] = total

    def drain_hops(step, carry):
        for stream in range(streams):
            for way in range(2):
                hop(way, step, stream).wait_send()
        return carry

    def drain_shares(step, carry):
        for stream in range(streams):
            for way in range(2):
                share(way, step, stream).wait_send()
        return carry

    lax.fori_loop(0, count - 1, drain_hops, 0)
    lax.fori_loop(0, count, drain_shares, 0)


def ring_scatter(grads, devices):
    count = devices // 2
    streams = len(grads)
    rows = grads[0].shape[0] // devices
    half = rows // 2
    widths = [grad.shape[1] for grad in grads]
    vmem = pl.BlockSpec(memory_space=pltpu.VMEM)
    return pl.pallas_call(
        functools.partial(scatter_kernel, count, streams),
        out_shape=[jax.ShapeDtypeStruct((rows, width), jnp.float32) for width in widths],
        in_specs=[vmem] * streams,
        out_specs=[vmem] * streams,
        scratch_shapes=[pltpu.VMEM((2, count, half, width), jnp.bfloat16) for width in widths]
        + [pltpu.VMEM((2, count - 1, half, width), jnp.bfloat16) for width in widths] * 2
        + [pltpu.SemaphoreType.DMA((streams, 2, count - 1))] * 2
        + [pltpu.SemaphoreType.DMA((streams, 2, count))] * 2,
        compiler_params=pltpu.CompilerParams(
            collective_id=1, has_side_effects=True, vmem_limit_bytes=40 * 1024 * 1024
        ),
        name="ring_scatter",
    )(*grads)


def turn(values, cos_table, sin_table, low_half):
    half = HEAD_HALF
    swapped = jnp.where(
        low_half, pltpu.roll(values, LANES - half, 1), pltpu.roll(values, half, 1)
    )
    return values * cos_table + swapped * sin_table


HEAD_HALF = 32


def lane_masks(rows):
    lane = lax.broadcasted_iota(jnp.int32, (rows, LANES), 1)
    return (lane % (2 * HEAD_HALF) < HEAD_HALF, lane < 2 * HEAD_HALF)


def allowed_pairs(pos_col, pos_row, seg_col, seg_row):
    near = jnp.abs(pos_col[...] - pos_row[...]) <= HALO
    return near & (seg_col[...] == seg_row[...])


def head_probs(queries, keys, allowed, scale):
    scores = (
        lax.dot_general(
            queries, keys, (((1,), (1,)), ((), ())), preferred_element_type=jnp.float32
        )
        * scale
    )
    scores = jnp.where(allowed, scores, NEG_FILL)
    top_score = jnp.max(scores, axis=-1, keepdims=True)
    total = jnp.sum(jnp.exp(scores - top_score), axis=-1, keepdims=True)
    return jnp.exp(scores - (top_score + jnp.log(total)))


def attend_kernel(
    scale, width, proj, cos_ref, sin_ref, pos_col, pos_row, seg_col, seg_row, qkv_out, mixed_out
):
    rows = proj.shape[0]
    low_half, first = lane_masks(rows)
    cos_table, sin_table = cos_ref[...], sin_ref[...]
    allowed = allowed_pairs(pos_col, pos_row, seg_col, seg_row)
    for start in range(0, width, LANES):
        queries = turn(proj[:, start : start + LANES], cos_table, sin_table, low_half)
        keys = turn(
            proj[:, width + start : width + start + LANES], cos_table, sin_table, low_half
        ).astype(jnp.bfloat16)
        values = proj[:, 2 * width + start : 2 * width + start + LANES]
        qkv_out[:, start : start + LANES] = queries.astype(jnp.bfloat16)
        qkv_out[:, width + start : width + start + LANES] = keys
        qkv_out[:, 2 * width + start : 2 * width + start + LANES] = values.astype(jnp.bfloat16)
        mixed = jnp.zeros((rows, LANES), jnp.float32)
        for head in range(2):
            mine = first if head == 0 else ~first
            probs = head_probs(
                jnp.where(mine, queries, 0.0).astype(jnp.bfloat16), keys, allowed, scale
            ).astype(jnp.bfloat16)
            mixed = mixed + jnp.dot(
                probs,
                jnp.where(mine, values, 0.0).astype(jnp.bfloat16),
                preferred_element_type=jnp.float32,
            )
        mixed_out[:, start : start + LANES] = mixed.astype(jnp.bfloat16)


def attend_back_kernel(
    scale,
    width,
    qkv,
    mixed_ref,
    dmixed_ref,
    cos_ref,
    sin_ref,
    pos_col,
    pos_row,
    seg_col,
    seg_row,
    dqkv_out,
):
    rows = qkv.shape[0]
    low_half, first = lane_masks(rows)
    cos_table, sin_table = cos_ref[...], -sin_ref[...]
    allowed = allowed_pairs(pos_col, pos_row, seg_col, seg_row)
    over_rows = (((0,), (0,)), ((), ()))
    over_lanes = (((1,), (1,)), ((), ()))
    for start in range(0, width, LANES):
        queries = qkv[:, start : start + LANES].astype(jnp.float32)
        keys = qkv[:, width + start : width + start + LANES]
        keys32 = keys.astype(jnp.float32)
        values = qkv[:, 2 * width + start : 2 * width + start + LANES]
        dmixed = dmixed_ref[:, start : start + LANES].astype(jnp.float32)
        products = dmixed * mixed_ref[:, start : start + LANES].astype(jnp.float32)
        dquery = jnp.zeros((rows, LANES), jnp.float32)
        dkey = jnp.zeros((rows, LANES), jnp.float32)
        dvalue = jnp.zeros((rows, LANES), jnp.float32)
        for head in range(2):
            mine = first if head == 0 else ~first
            head_queries = jnp.where(mine, queries, 0.0).astype(jnp.bfloat16)
            head_keys = jnp.where(mine, keys32, 0.0).astype(jnp.bfloat16)
            head_dmixed = jnp.where(mine, dmixed, 0.0).astype(jnp.bfloat16)
            delta = jnp.sum(jnp.where(mine, products, 0.0), axis=-1, keepdims=True)
            probs = head_probs(head_queries, keys, allowed, scale)
            dprobs = lax.dot_general(
                head_dmixed, values, over_lanes, preferred_element_type=jnp.float32
            )
            dscores = (probs * (dprobs - delta) * scale).astype(jnp.bfloat16)
            dvalue = dvalue + lax.dot_general(
                probs.astype(jnp.bfloat16),
                head_dmixed,
                over_rows,
                preferred_element_type=jnp.float32,
            )
            dkey = dkey + lax.dot_general(
                dscores, head_queries, over_rows, preferred_element_type=jnp.float32
            )
            dquery = dquery + jnp.dot(dscores, head_keys, preferred_element_type=jnp.float32)
        dquery = turn(dquery, cos_table, sin_table, low_half)
        dkey = turn(dkey, cos_table, sin_table, low_half)
        dqkv_out[:, start : start + LANES] = dquery.astype(jnp.bfloat16)
        dqkv_out[:, width + start : width + start + LANES] = dkey.astype(jnp.bfloat16)
        dqkv_out[:, 2 * width + start : 2 * width + start + LANES] = dvalue.astype(jnp.bfloat16)


def local_call(kernel, name, out_shape, operands, flops):
    vmem = pl.BlockSpec(memory_space=pltpu.VMEM)
    single = not isinstance(out_shape, list)
    return pl.pallas_call(
        kernel,
        out_shape=out_shape,
        in_specs=[vmem] * len(operands),
        out_specs=vmem if single else [vmem] * len(out_shape),
        cost_estimate=pl.CostEstimate(
            flops=flops, bytes_accessed=4 * 1024 * 1024, transcendentals=flops // 256
        ),
        compiler_params=pltpu.CompilerParams(vmem_limit_bytes=32 * 1024 * 1024),
        name=name,
    )(*operands)


class PairedAttention:
    def __init__(self, positions, segments, head_size, width):
        rows = positions.shape[0]
        cos_table, sin_table = rotary_tables(positions, head_size)
        cos_table, sin_table = cos_table[:, 0, :], sin_table[:, 0, :]
        self.width = width
        self.scale = 1.0 / math.sqrt(head_size)
        self.flops = 2 * rows * rows * LANES * (width // head_size)
        self.shared = (
            jnp.concatenate([cos_table] * 4, axis=1),
            jnp.concatenate([-sin_table, sin_table] * 2, axis=1),
            positions[:, None],
            positions[None, :],
            segments[:, None],
            segments[None, :],
        )

    def forward(self, projected):
        rows = projected.shape[0]
        self.qkv, self.mixed = local_call(
            functools.partial(attend_kernel, self.scale, self.width),
            "attend",
            [
                jax.ShapeDtypeStruct((rows, 3 * self.width), jnp.bfloat16),
                jax.ShapeDtypeStruct((rows, self.width), jnp.bfloat16),
            ],
            (projected,) + self.shared,
            2 * self.flops,
        )
        return self.mixed

    def backward(self, dmixed):
        rows = dmixed.shape[0]
        return local_call(
            functools.partial(attend_back_kernel, self.scale, self.width),
            "attend_back",
            jax.ShapeDtypeStruct((rows, 3 * self.width), jnp.bfloat16),
            (self.qkv, self.mixed, dmixed) + self.shared,
            5 * self.flops,
        )


class BlockAttention:
    def __init__(self, positions, segments, head_size, width):
        self.total_len = positions.shape[0]
        self.segments = segments
        self.head_size = head_size
        self.width = width
        self.scale = 1.0 / math.sqrt(head_size)
        self.cos_table, self.sin_table = rotary_tables(positions, head_size)

    def heads(self, values):
        return values.reshape(self.total_len, self.width // self.head_size, self.head_size)

    def forward(self, projected):
        width, total_len = self.width, self.total_len
        self.block_rows = min(total_len, 512)
        self.slab_rows = self.block_rows + 2 * HALO
        tables = (self.cos_table, self.sin_table)
        self.queries = rotate(self.heads(projected[:, :width]), *tables).astype(jnp.bfloat16)
        keys = rotate(self.heads(projected[:, width : 2 * width]), *tables).astype(jnp.bfloat16)
        values = self.heads(projected[:, 2 * width :]).astype(jnp.bfloat16)
        pad_spec = ((HALO, HALO), (0, 0), (0, 0))
        self.key_pad = jnp.pad(keys, pad_spec)
        self.value_pad = jnp.pad(values, pad_spec)
        seg_pad = jnp.pad(self.segments, (HALO, HALO), constant_values=-1)
        mixed_parts = []
        self.logsums = []
        self.masks = []
        for start in range(0, total_len, self.block_rows):
            own = slice(start, start + self.block_rows)
            slab = slice(start, start + self.slab_rows)
            allowed = window_mask(
                start + jnp.arange(self.block_rows, dtype=jnp.int32),
                start - HALO + jnp.arange(self.slab_rows, dtype=jnp.int32),
                self.segments[own],
                seg_pad[slab],
                HALO,
                total_len,
            )
            mixed, logsum = attend_block(
                self.queries[own], self.key_pad[slab], self.value_pad[slab], allowed, self.scale
            )
            self.masks.append(allowed)
            self.logsums.append(logsum)
            mixed_parts.append(mixed)
        self.mixed = jnp.concatenate(mixed_parts, axis=0).astype(jnp.bfloat16)
        return self.mixed.reshape(total_len, width)

    def backward(self, dmixed):
        total_len = self.total_len
        dmixed = self.heads(dmixed)
        padded = (total_len + 2 * HALO,) + dmixed.shape[1:]
        dkey_pad = jnp.zeros(padded, jnp.float32)
        dvalue_pad = jnp.zeros(padded, jnp.float32)
        dquery_parts = []
        for index, start in enumerate(range(0, total_len, self.block_rows)):
            own = slice(start, start + self.block_rows)
            slab = slice(start, start + self.slab_rows)
            dqueries, dkeys, dvalues = attend_back(
                self.queries[own],
                self.key_pad[slab],
                self.value_pad[slab],
                self.masks[index],
                self.scale,
                self.logsums[index],
                self.mixed[own],
                dmixed[own],
            )
            dquery_parts.append(dqueries)
            dkey_pad = dkey_pad.at[slab].add(dkeys)
            dvalue_pad = dvalue_pad.at[slab].add(dvalues)
        inner = slice(HALO, HALO + total_len)
        tables = (self.cos_table, self.sin_table)
        parts = [
            unrotate(jnp.concatenate(dquery_parts, axis=0), *tables),
            unrotate(dkey_pad[inner], *tables),
            dvalue_pad[inner],
        ]
        return jnp.concatenate(
            [part.reshape(total_len, self.width) for part in parts], axis=1
        ).astype(jnp.bfloat16)


def dot(left, right, left_dim, right_dim):
    return lax.dot_general(
        left,
        right,
        (((left_dim,), (right_dim,)), ((), ())),
        preferred_element_type=jnp.float32,
    )


def padded_to_lanes(values):
    return jnp.pad(values, ((0, 0), (0, -values.shape[1] % LANES)))


def high_and_low(gain):
    high = gain.astype(jnp.bfloat16)
    return [high[:, None], (gain - high.astype(jnp.float32)).astype(jnp.bfloat16)[:, None]]


def per_device(
    devices,
    seq_size,
    tokens,
    segments,
    cotangent,
    qkv_weight,
    out_weight,
    in_weight,
    down_weight,
    attn_gain,
    mlp_gain,
):
    layer_in = tokens[0]
    seg_local = segments[0]
    cot_local = cotangent[0]
    own_rows, model_width = layer_in.shape
    head_size = model_width // HEADS
    local_width = qkv_weight.shape[2]
    local_hidden = in_weight.shape[2]
    shard_rows = qkv_weight.shape[0]
    total_len = own_rows * seq_size
    paired = (
        seq_size == 2
        and total_len <= 512
        and local_width % LANES == 0
        and head_size == 2 * HEAD_HALF
    )
    swap = [(0, 1), (1, 0)]

    def rows_of_all(values):
        if paired:
            return jnp.concatenate([values, lax.ppermute(values, "seq", swap)], axis=0)
        return lax.all_gather(values, "seq", axis=0, tiled=True)

    def sum_to_owner(partial):
        if paired:
            other = lax.ppermute(partial[own_rows:].astype(jnp.bfloat16), "seq", swap)
            return partial[:own_rows] + other.astype(jnp.float32)
        return lax.psum_scatter(
            partial.astype(jnp.bfloat16), "seq", scatter_dimension=0, tiled=True
        ).astype(jnp.float32)

    def sum_over_seq(part):
        if paired:
            return part + lax.ppermute(part, "seq", swap)
        return lax.psum(part, "seq")

    first_pack = jnp.concatenate(
        [qkv_weight.reshape(shard_rows, 3 * local_width), out_weight.T]
        + [
            padded_to_lanes(
                jnp.concatenate(high_and_low(attn_gain) + high_and_low(mlp_gain), axis=1)
            )
        ],
        axis=1,
    )
    second_pack = jnp.concatenate(
        [
            padded_to_lanes(in_weight[:, 0, :]),
            padded_to_lanes(in_weight[:, 1, :]),
            padded_to_lanes(down_weight.T),
        ],
        axis=1,
    )
    wide = second_pack.shape[1] // 3
    first_full, second_full = ring_gather([first_pack, second_pack], devices)
    full_qkv = first_full[:, : 3 * local_width]
    full_out = first_full[:, 3 * local_width : 4 * local_width]
    gains = first_full[:, 4 * local_width : 4 * local_width + 4].astype(jnp.float32)
    gain_attn = gains[:, 0] + gains[:, 1]
    gain_mlp = gains[:, 2] + gains[:, 3]
    full_in = second_full[:, : 2 * wide]
    full_down = second_full[:, 2 * wide :]

    inputs32 = layer_in.astype(jnp.float32)
    all_inputs32 = rows_of_all(layer_in).astype(jnp.float32)
    cot_full = rows_of_all(cot_local)
    normed_full = norm_forward(all_inputs32, gain_attn)[0].astype(jnp.bfloat16)
    unit_one, inv_one = norm_forward(inputs32, gain_attn)[1:]
    if paired:
        seg_full = rows_of_all(
            jnp.broadcast_to(seg_local.astype(jnp.float32)[:, None], (own_rows, LANES))
        )[:, 0].astype(jnp.int32)
        place = lax.axis_index("seq")
        arange = jnp.arange(own_rows, dtype=jnp.int32)
        positions = jnp.concatenate(
            [place * own_rows + arange, (1 - place) * own_rows + arange], axis=0
        )
        attention = PairedAttention(positions, seg_full, head_size, local_width)
    else:
        seg_full = rows_of_all(seg_local.astype(jnp.bfloat16)).astype(jnp.int32)
        positions = jnp.arange(total_len, dtype=jnp.int32)
        attention = BlockAttention(positions, seg_full, head_size, local_width)

    mixed = attention.forward(dot(normed_full, full_qkv, 1, 0))
    residual = inputs32 + sum_to_owner(dot(mixed, full_out, 1, 1))
    normed_two, unit_two, inv_two = norm_forward(residual, gain_mlp)
    normed_two_full = rows_of_all(normed_two.astype(jnp.bfloat16))
    expanded = dot(normed_two_full, full_in, 1, 0)
    gate_in = expanded[:, :wide]
    linear_in = expanded[:, wide:]
    activated = gelu_value(gate_in)
    middle_b = (activated * linear_in).astype(jnp.bfloat16)
    layer_out = (residual + sum_to_owner(dot(middle_b, full_down, 1, 1))).astype(jnp.bfloat16)

    down_grad = dot(cot_full, middle_b, 0, 0).astype(jnp.bfloat16)
    dmiddle = dot(cot_full, full_down, 1, 0)
    dexpanded_b = jnp.concatenate(
        [dmiddle * linear_in * gelu_slope(gate_in), dmiddle * activated], axis=1
    ).astype(jnp.bfloat16)
    dnormed_two = sum_to_owner(dot(dexpanded_b, full_in, 1, 1))
    in_grad = dot(normed_two_full, dexpanded_b, 0, 0).astype(jnp.bfloat16)
    dres_norm, mlp_gain_part = norm_backward(dnormed_two, gain_mlp, unit_two, inv_two)
    dresidual = cot_local.astype(jnp.float32) + dres_norm
    dres_full = rows_of_all(dresidual.astype(jnp.bfloat16))
    dmixed = dot(dres_full, full_out, 1, 0).astype(jnp.bfloat16)
    out_grad = dot(dres_full, mixed, 0, 0).astype(jnp.bfloat16)
    dqkv_b = attention.backward(dmixed)
    dnormed_one = sum_to_owner(dot(dqkv_b, full_qkv, 1, 1))
    qkv_grad = dot(normed_full, dqkv_b, 0, 0).astype(jnp.bfloat16)
    dinput_norm, attn_gain_part = norm_backward(dnormed_one, gain_attn, unit_one, inv_one)
    tokens_grad = (dresidual + dinput_norm).astype(jnp.bfloat16)
    gain_sums = sum_over_seq(jnp.stack([attn_gain_part, mlp_gain_part]))
    gain_grad = padded_to_lanes(gain_sums.T).astype(jnp.bfloat16)

    in_share, qkv_share, down_share, out_share, gain_share = ring_scatter(
        [in_grad, qkv_grad, down_grad, out_grad, gain_grad], devices
    )
    return (
        layer_out[None],
        tokens_grad[None],
        qkv_share.reshape(shard_rows, 3, local_width),
        out_share.T,
        jnp.stack([in_share[:, :local_hidden], in_share[:, wide : wide + local_hidden]], axis=1),
        down_share[:, :local_hidden].T,
        gain_share[:, 0],
        gain_share[:, 1],
    )


def solution(mesh):
    return jax.shard_map(
        functools.partial(per_device, mesh.shape["dp"], mesh.shape["seq"]),
        mesh=mesh,
        in_specs=(
            P("dp", "seq", None),
            P("dp", "seq"),
            P("dp", "seq", None),
            P("dp", None, "seq"),
            P("seq", "dp"),
            P("dp", None, "seq"),
            P("seq", "dp"),
            P("dp"),
            P("dp"),
        ),
        out_specs=(
            P("dp", "seq", None),
            P("dp", "seq", None),
            P("dp", None, "seq"),
            P("seq", "dp"),
            P("dp", None, "seq"),
            P("seq", "dp"),
            P("dp"),
            P("dp"),
        ),
        check_vma=False,
    )
```

```python
import functools
import math

import jax
import jax.numpy as jnp
from jax import lax
from jax.experimental import pallas as pl
from jax.experimental.pallas import tpu as pltpu
from jax.sharding import PartitionSpec as P

HEADS = 16
HALO = 64


EPS = 1e-05
THETA = 10000.0
NEG_FILL = -1e30


def norm_forward(values, gain):
    center = values - jnp.mean(values, axis=-1, keepdims=True)
    inv_std = lax.rsqrt(jnp.mean(center * center, axis=-1, keepdims=True) + EPS)
    unit_rows = center * inv_std
    return (unit_rows * gain, unit_rows, inv_std)


def norm_backward(grad_rows, gain, unit_rows, inv_std):
    scaled = grad_rows * gain
    inner = (
        scaled
        - jnp.mean(scaled, axis=-1, keepdims=True)
        - unit_rows * jnp.mean(scaled * unit_rows, axis=-1, keepdims=True)
    )
    return (inner * inv_std, jnp.sum(grad_rows * unit_rows, axis=0))


def gelu_value(inputs):
    return 0.5 * inputs * (1.0 + lax.erf(inputs * 0.7071067811865476))


def gelu_slope(inputs):
    return (
        0.5 * (1.0 + lax.erf(inputs * 0.7071067811865476))
        + inputs * jnp.exp(-0.5 * inputs * inputs) * 0.3989422804014327
    )


def rotary_tables(positions, head_size):
    half_size = head_size // 2
    freqs = jnp.power(THETA, -(2.0 / head_size) * jnp.arange(half_size, dtype=jnp.float32))
    angles = positions.astype(jnp.float32)[:, None] * freqs[None, :]
    return (jnp.cos(angles)[:, None, :], jnp.sin(angles)[:, None, :])


def rotate(values, cos_table, sin_table):
    half_size = values.shape[-1] // 2
    lower_half = values[..., :half_size]
    upper_half = values[..., half_size:]
    return jnp.concatenate(
        [
            lower_half * cos_table - upper_half * sin_table,
            upper_half * cos_table + lower_half * sin_table,
        ],
        axis=-1,
    )


def unrotate(grads, cos_table, sin_table):
    half_size = grads.shape[-1] // 2
    lower_half = grads[..., :half_size]
    upper_half = grads[..., half_size:]
    return jnp.concatenate(
        [
            lower_half * cos_table + upper_half * sin_table,
            upper_half * cos_table - lower_half * sin_table,
        ],
        axis=-1,
    )


def window_mask(query_pos, key_pos, query_seg, key_seg, halo_width, total_len):
    near = jnp.abs(query_pos[:, None] - key_pos[None, :]) <= halo_width
    inside = (key_pos >= 0) & (key_pos < total_len)
    return near & inside[None, :] & (query_seg[:, None] == key_seg[None, :])


def block_scores(queries, key_slab, allowed, scale):
    scores = (
        jnp.einsum("qhd,khd->hqk", queries, key_slab, preferred_element_type=jnp.float32) * scale
    )
    return jnp.where(allowed[None], scores, NEG_FILL)


def attend_block(queries, key_slab, value_slab, allowed, scale):
    scores = block_scores(queries, key_slab, allowed, scale)
    top_score = jnp.max(scores, axis=-1, keepdims=True)
    total = jnp.sum(jnp.exp(scores - top_score), axis=-1, keepdims=True)
    logsum = top_score + jnp.log(total)
    probs = jnp.exp(scores - logsum).astype(jnp.bfloat16)
    mixed = jnp.einsum("hqk,khd->qhd", probs, value_slab, preferred_element_type=jnp.float32)
    return (mixed, logsum[..., 0])


def attend_back(queries, key_slab, value_slab, allowed, scale, logsum, mixed_b, dmixed_b):
    scores = block_scores(queries, key_slab, allowed, scale)
    probs = jnp.exp(scores - logsum[..., None])
    probs_b = probs.astype(jnp.bfloat16)
    dvalues = jnp.einsum("hqk,qhd->khd", probs_b, dmixed_b, preferred_element_type=jnp.float32)
    dprobs = jnp.einsum("qhd,khd->hqk", dmixed_b, value_slab, preferred_element_type=jnp.float32)
    delta = jnp.transpose(
        jnp.sum(dmixed_b.astype(jnp.float32) * mixed_b.astype(jnp.float32), axis=-1)
    )
    dscores = (probs * (dprobs - delta[..., None]) * scale).astype(jnp.bfloat16)
    dqueries = jnp.einsum("hqk,khd->qhd", dscores, key_slab, preferred_element_type=jnp.float32)
    dkeys = jnp.einsum("hqk,qhd->khd", dscores, queries, preferred_element_type=jnp.float32)
    return (dqueries, dkeys, dvalues)


MESH = pl.DeviceIdType.MESH
VMEM_LIMIT = 60 * 1024 * 1024
LANES = 128


def ring_place(count):
    me = lax.axis_index("dp")
    core = me % 2
    chip = me // 2
    row, column = chip // 2, chip % 2
    place = (1 - column) * row + column * (count - 1 - row)
    return (core, place)


def chip_at(place, count):
    side = place // (count // 2)
    return (1 - side) * (2 * place) + side * (2 * (count - 1 - place) + 1)


def neighbours(core, place, count):
    right = chip_at((place + 1) % count, count) * 2 + core
    left = chip_at((place + count - 1) % count, count) * 2 + core
    return (right, left, lax.axis_index("dp") + 1 - 2 * core)


def greet(devices):
    barrier = pltpu.get_barrier_semaphore()
    for device in devices:
        pl.semaphore_signal(barrier, inc=1, device_id={"dp": device}, device_id_type=MESH)
    pl.semaphore_wait(barrier, len(devices))


def gather_kernel(count, streams, *refs):
    shards = refs[:streams]
    fulls = refs[streams : 2 * streams]
    own_sem, send_sem, recv_sem, pair_send, pair_recv = refs[2 * streams :]
    rows = shards[0].shape[0]
    half = rows // 2
    core, place = ring_place(count)
    right, left, partner = neighbours(core, place, count)
    targets = (right, left)
    lanes = [(way, stream) for stream in range(streams) for way in range(2)]

    def piece(way, step, stream):
        shift = count - step if way == 0 else step
        owner = chip_at((place + shift) % count, count) * 2 + core
        start = pl.multiple_of(owner * rows + way * half, half)
        return fulls[stream].at[pl.ds(start, half)]

    def hop(way, step, stream):
        ref = piece(way, step, stream)
        return pltpu.make_async_remote_copy(
            src_ref=ref,
            dst_ref=ref,
            send_sem=send_sem.at[stream, way, step],
            recv_sem=recv_sem.at[stream, way, step],
            device_id={"dp": targets[way]},
            device_id_type=MESH,
        )

    def share(way, step, stream):
        ref = piece(way, step, stream)
        return pltpu.make_async_remote_copy(
            src_ref=ref,
            dst_ref=ref,
            send_sem=pair_send.at[stream, way, step],
            recv_sem=pair_recv.at[stream, way, step],
            device_id={"dp": partner},
            device_id_type=MESH,
        )

    me = lax.axis_index("dp")
    owns = [
        pltpu.make_async_copy(
            shards[stream],
            fulls[stream].at[pl.ds(pl.multiple_of(me * rows, rows), rows)],
            own_sem.at[stream],
        )
        for stream in range(streams)
    ]
    for own in owns:
        own.start()
    greet((right, left, partner))
    for own in owns:
        own.wait()
    for way, stream in lanes:
        hop(way, 0, stream).start()
        share(way, 0, stream).start()

    def step_body(step, carry):
        for way, stream in lanes:
            hop(way, step - 1, stream).wait_recv()
            hop(way, step, stream).start()
            share(way, step, stream).start()
        return carry

    lax.fori_loop(1, count - 1, step_body, 0)
    for way, stream in lanes:
        hop(way, count - 2, stream).wait_recv()
        share(way, count - 1, stream).start()

    def drain_hops(step, carry):
        for way, stream in lanes:
            hop(way, step, stream).wait_send()
        return carry

    def drain_shares(step, carry):
        for way, stream in lanes:
            share(way, step, stream).wait_send()
            share(way, step, stream).wait_recv()
        return carry

    lax.fori_loop(0, count - 1, drain_hops, 0)
    lax.fori_loop(0, count, drain_shares, 0)


def ring_gather(shards, devices):
    count = devices // 2
    streams = len(shards)
    return pl.pallas_call(
        functools.partial(gather_kernel, count, streams),
        out_shape=[
            jax.ShapeDtypeStruct((devices * shard.shape[0], shard.shape[1]), shard.dtype)
            for shard in shards
        ],
        in_specs=[pl.BlockSpec(memory_space=pltpu.VMEM)] * streams,
        out_specs=[pl.BlockSpec(memory_space=pl.ANY)] * streams,
        scratch_shapes=[pltpu.SemaphoreType.DMA((streams,))]
        + [pltpu.SemaphoreType.DMA((streams, 2, count - 1))] * 2
        + [pltpu.SemaphoreType.DMA((streams, 2, count))] * 2,
        cost_estimate=pl.CostEstimate(
            flops=0, bytes_accessed=128 * 1024 * 1024, transcendentals=0
        ),
        compiler_params=pltpu.CompilerParams(
            collective_id=0, has_side_effects=True, vmem_limit_bytes=VMEM_LIMIT
        ),
        name="ring_gather",
    )(*shards)


def scatter_kernel(count, streams, *refs):
    grads = refs[:streams]
    outs = refs[streams : 2 * streams]
    pairs = refs[2 * streams : 3 * streams]
    sends = refs[3 * streams : 4 * streams]
    recvs = refs[4 * streams : 5 * streams]
    send_sem, recv_sem, pair_send, pair_recv = refs[5 * streams :]
    rows = outs[0].shape[0]
    half = rows // 2
    core, place = ring_place(count)
    right, left, partner = neighbours(core, place, count)
    targets = (right, left)

    def block(way, step, which):
        shift = 2 * count - 1 - step if way == 0 else 1 + step
        owner = chip_at((place + shift) % count, count) * 2 + which
        return pl.ds(pl.multiple_of(owner * rows + way * half, half), half)

    def share(way, step, stream):
        return pltpu.make_async_remote_copy(
            src_ref=grads[stream].at[block(way, step, 1 - core)],
            dst_ref=pairs[stream].at[way, step],
            send_sem=pair_send.at[stream, way, step],
            recv_sem=pair_recv.at[stream, way, step],
            device_id={"dp": partner},
            device_id_type=MESH,
        )

    def hop(way, step, stream):
        return pltpu.make_async_remote_copy(
            src_ref=sends[stream].at[way, step],
            dst_ref=recvs[stream].at[way, step],
            send_sem=send_sem.at[stream, way, step],
            recv_sem=recv_sem.at[stream, way, step],
            device_id={"dp": targets[way]},
            device_id_type=MESH,
        )

    def pair_sum(way, step, stream):
        share(way, step, stream).wait_recv()
        own = grads[stream][block(way, step, core), :].astype(jnp.float32)
        return own + pairs[stream][way, step].astype(jnp.float32)

    greet((right, left, partner))

    def start_shares(step, carry):
        for stream in range(streams):
            for way in range(2):
                share(way, step, stream).start()
        return carry

    lax.fori_loop(0, count, start_shares, 0)
    for stream in range(streams):
        for way in range(2):
            sends[stream][way, 0] = pair_sum(way, 0, stream).astype(jnp.bfloat16)
            hop(way, 0, stream).start()

    def step_body(step, carry):
        for stream in range(streams):
            for way in range(2):
                total = pair_sum(way, step, stream)
                hop(way, step - 1, stream).wait_recv()
                total = total + recvs[stream][way, step - 1].astype(jnp.float32)
                sends[stream][way, step] = total.astype(jnp.bfloat16)
                hop(way, step, stream).start()
        return carry

    lax.fori_loop(1, count - 1, step_body, 0)
    for stream in range(streams):
        for way in range(2):
            total = pair_sum(way, count - 1, stream)
            hop(way, count - 2, stream).wait_recv()
            total = total + recvs[stream][way, count - 2].astype(jnp.float32)
            outs[stream][way * half : (way + 1) * half, :] = total

    def drain_hops(step, carry):
        for stream in range(streams):
            for way in range(2):
                hop(way, step, stream).wait_send()
        return carry

    def drain_shares(step, carry):
        for stream in range(streams):
            for way in range(2):
                share(way, step, stream).wait_send()
        return carry

    lax.fori_loop(0, count - 1, drain_hops, 0)
    lax.fori_loop(0, count, drain_shares, 0)


def ring_scatter(grads, devices):
    count = devices // 2
    streams = len(grads)
    rows = grads[0].shape[0] // devices
    half = rows // 2
    widths = [grad.shape[1] for grad in grads]
    vmem = pl.BlockSpec(memory_space=pltpu.VMEM)
    return pl.pallas_call(
        functools.partial(scatter_kernel, count, streams),
        out_shape=[jax.ShapeDtypeStruct((rows, width), jnp.float32) for width in widths],
        in_specs=[vmem] * streams,
        out_specs=[vmem] * streams,
        scratch_shapes=[pltpu.VMEM((2, count, half, width), jnp.bfloat16) for width in widths]
        + [pltpu.VMEM((2, count - 1, half, width), jnp.bfloat16) for width in widths] * 2
        + [pltpu.SemaphoreType.DMA((streams, 2, count - 1))] * 2
        + [pltpu.SemaphoreType.DMA((streams, 2, count))] * 2,
        compiler_params=pltpu.CompilerParams(
            collective_id=1, has_side_effects=True, vmem_limit_bytes=40 * 1024 * 1024
        ),
        name="ring_scatter",
    )(*grads)


def turn(values, cos_table, sin_table, low_half):
    half = HEAD_HALF
    swapped = jnp.where(
        low_half, pltpu.roll(values, LANES - half, 1), pltpu.roll(values, half, 1)
    )
    return values * cos_table + swapped * sin_table


HEAD_HALF = 32


def lane_masks(rows):
    lane = lax.broadcasted_iota(jnp.int32, (rows, LANES), 1)
    return (lane % (2 * HEAD_HALF) < HEAD_HALF, lane < 2 * HEAD_HALF)


def allowed_pairs(pos_col, pos_row, seg_col, seg_row):
    near = jnp.abs(pos_col[...] - pos_row[...]) <= HALO
    return near & (seg_col[...] == seg_row[...])


def head_probs(queries, keys, allowed, scale):
    scores = (
        lax.dot_general(
            queries, keys, (((1,), (1,)), ((), ())), preferred_element_type=jnp.float32
        )
        * scale
    )
    scores = jnp.where(allowed, scores, NEG_FILL)
    top_score = jnp.max(scores, axis=-1, keepdims=True)
    total = jnp.sum(jnp.exp(scores - top_score), axis=-1, keepdims=True)
    return jnp.exp(scores - (top_score + jnp.log(total)))


def attend_kernel(
    scale, width, proj, cos_ref, sin_ref, pos_col, pos_row, seg_col, seg_row, qkv_out, mixed_out
):
    rows = proj.shape[0]
    low_half, first = lane_masks(rows)
    cos_table, sin_table = cos_ref[...], sin_ref[...]
    allowed = allowed_pairs(pos_col, pos_row, seg_col, seg_row)
    for start in range(0, width, LANES):
        queries = turn(proj[:, start : start + LANES], cos_table, sin_table, low_half)
        keys = turn(
            proj[:, width + start : width + start + LANES], cos_table, sin_table, low_half
        ).astype(jnp.bfloat16)
        values = proj[:, 2 * width + start : 2 * width + start + LANES]
        qkv_out[:, start : start + LANES] = queries.astype(jnp.bfloat16)
        qkv_out[:, width + start : width + start + LANES] = keys
        qkv_out[:, 2 * width + start : 2 * width + start + LANES] = values.astype(jnp.bfloat16)
        mixed = jnp.zeros((rows, LANES), jnp.float32)
        for head in range(2):
            mine = first if head == 0 else ~first
            probs = head_probs(
                jnp.where(mine, queries, 0.0).astype(jnp.bfloat16), keys, allowed, scale
            ).astype(jnp.bfloat16)
            mixed = mixed + jnp.dot(
                probs,
                jnp.where(mine, values, 0.0).astype(jnp.bfloat16),
                preferred_element_type=jnp.float32,
            )
        mixed_out[:, start : start + LANES] = mixed.astype(jnp.bfloat16)


def attend_back_kernel(
    scale,
    width,
    qkv,
    mixed_ref,
    dmixed_ref,
    cos_ref,
    sin_ref,
    pos_col,
    pos_row,
    seg_col,
    seg_row,
    dqkv_out,
):
    rows = qkv.shape[0]
    low_half, first = lane_masks(rows)
    cos_table, sin_table = cos_ref[...], -sin_ref[...]
    allowed = allowed_pairs(pos_col, pos_row, seg_col, seg_row)
    over_rows = (((0,), (0,)), ((), ()))
    over_lanes = (((1,), (1,)), ((), ()))
    for start in range(0, width, LANES):
        queries = qkv[:, start : start + LANES].astype(jnp.float32)
        keys = qkv[:, width + start : width + start + LANES]
        keys32 = keys.astype(jnp.float32)
        values = qkv[:, 2 * width + start : 2 * width + start + LANES]
        dmixed = dmixed_ref[:, start : start + LANES].astype(jnp.float32)
        products = dmixed * mixed_ref[:, start : start + LANES].astype(jnp.float32)
        dquery = jnp.zeros((rows, LANES), jnp.float32)
        dkey = jnp.zeros((rows, LANES), jnp.float32)
        dvalue = jnp.zeros((rows, LANES), jnp.float32)
        for head in range(2):
            mine = first if head == 0 else ~first
            head_queries = jnp.where(mine, queries, 0.0).astype(jnp.bfloat16)
            head_keys = jnp.where(mine, keys32, 0.0).astype(jnp.bfloat16)
            head_dmixed = jnp.where(mine, dmixed, 0.0).astype(jnp.bfloat16)
            delta = jnp.sum(jnp.where(mine, products, 0.0), axis=-1, keepdims=True)
            probs = head_probs(head_queries, keys, allowed, scale)
            dprobs = lax.dot_general(
                head_dmixed, values, over_lanes, preferred_element_type=jnp.float32
            )
            dscores = (probs * (dprobs - delta) * scale).astype(jnp.bfloat16)
            dvalue = dvalue + lax.dot_general(
                probs.astype(jnp.bfloat16),
                head_dmixed,
                over_rows,
                preferred_element_type=jnp.float32,
            )
            dkey = dkey + lax.dot_general(
                dscores, head_queries, over_rows, preferred_element_type=jnp.float32
            )
            dquery = dquery + jnp.dot(dscores, head_keys, preferred_element_type=jnp.float32)
        dquery = turn(dquery, cos_table, sin_table, low_half)
        dkey = turn(dkey, cos_table, sin_table, low_half)
        dqkv_out[:, start : start + LANES] = dquery.astype(jnp.bfloat16)
        dqkv_out[:, width + start : width + start + LANES] = dkey.astype(jnp.bfloat16)
        dqkv_out[:, 2 * width + start : 2 * width + start + LANES] = dvalue.astype(jnp.bfloat16)


def local_call(kernel, name, out_shape, operands, flops):
    vmem = pl.BlockSpec(memory_space=pltpu.VMEM)
    single = not isinstance(out_shape, list)
    return pl.pallas_call(
        kernel,
        out_shape=out_shape,
        in_specs=[vmem] * len(operands),
        out_specs=vmem if single else [vmem] * len(out_shape),
        cost_estimate=pl.CostEstimate(
            flops=flops, bytes_accessed=4 * 1024 * 1024, transcendentals=flops // 256
        ),
        compiler_params=pltpu.CompilerParams(vmem_limit_bytes=32 * 1024 * 1024),
        name=name,
    )(*operands)


class PairedAttention:
    def __init__(self, positions, segments, head_size, width):
        rows = positions.shape[0]
        cos_table, sin_table = rotary_tables(positions, head_size)
        cos_table, sin_table = cos_table[:, 0, :], sin_table[:, 0, :]
        self.width = width
        self.scale = 1.0 / math.sqrt(head_size)
        self.flops = 2 * rows * rows * LANES * (width // head_size)
        self.shared = (
            jnp.concatenate([cos_table] * 4, axis=1),
            jnp.concatenate([-sin_table, sin_table] * 2, axis=1),
            positions[:, None],
            positions[None, :],
            segments[:, None],
            segments[None, :],
        )

    def forward(self, projected):
        rows = projected.shape[0]
        self.qkv, self.mixed = local_call(
            functools.partial(attend_kernel, self.scale, self.width),
            "attend",
            [
                jax.ShapeDtypeStruct((rows, 3 * self.width), jnp.bfloat16),
                jax.ShapeDtypeStruct((rows, self.width), jnp.bfloat16),
            ],
            (projected,) + self.shared,
            2 * self.flops,
        )
        return self.mixed

    def backward(self, dmixed):
        rows = dmixed.shape[0]
        return local_call(
            functools.partial(attend_back_kernel, self.scale, self.width),
            "attend_back",
            jax.ShapeDtypeStruct((rows, 3 * self.width), jnp.bfloat16),
            (self.qkv, self.mixed, dmixed) + self.shared,
            5 * self.flops,
        )


class BlockAttention:
    def __init__(self, positions, segments, head_size, width):
        self.total_len = positions.shape[0]
        self.segments = segments
        self.head_size = head_size
        self.width = width
        self.scale = 1.0 / math.sqrt(head_size)
        self.cos_table, self.sin_table = rotary_tables(positions, head_size)

    def heads(self, values):
        return values.reshape(self.total_len, self.width // self.head_size, self.head_size)

    def forward(self, projected):
        width, total_len = self.width, self.total_len
        self.block_rows = min(total_len, 512)
        self.slab_rows = self.block_rows + 2 * HALO
        tables = (self.cos_table, self.sin_table)
        self.queries = rotate(self.heads(projected[:, :width]), *tables).astype(jnp.bfloat16)
        keys = rotate(self.heads(projected[:, width : 2 * width]), *tables).astype(jnp.bfloat16)
        values = self.heads(projected[:, 2 * width :]).astype(jnp.bfloat16)
        pad_spec = ((HALO, HALO), (0, 0), (0, 0))
        self.key_pad = jnp.pad(keys, pad_spec)
        self.value_pad = jnp.pad(values, pad_spec)
        seg_pad = jnp.pad(self.segments, (HALO, HALO), constant_values=-1)
        mixed_parts = []
        self.logsums = []
        self.masks = []
        for start in range(0, total_len, self.block_rows):
            own = slice(start, start + self.block_rows)
            slab = slice(start, start + self.slab_rows)
            allowed = window_mask(
                start + jnp.arange(self.block_rows, dtype=jnp.int32),
                start - HALO + jnp.arange(self.slab_rows, dtype=jnp.int32),
                self.segments[own],
                seg_pad[slab],
                HALO,
                total_len,
            )
            mixed, logsum = attend_block(
                self.queries[own], self.key_pad[slab], self.value_pad[slab], allowed, self.scale
            )
            self.masks.append(allowed)
            self.logsums.append(logsum)
            mixed_parts.append(mixed)
        self.mixed = jnp.concatenate(mixed_parts, axis=0).astype(jnp.bfloat16)
        return self.mixed.reshape(total_len, width)

    def backward(self, dmixed):
        total_len = self.total_len
        dmixed = self.heads(dmixed)
        padded = (total_len + 2 * HALO,) + dmixed.shape[1:]
        dkey_pad = jnp.zeros(padded, jnp.float32)
        dvalue_pad = jnp.zeros(padded, jnp.float32)
        dquery_parts = []
        for index, start in enumerate(range(0, total_len, self.block_rows)):
            own = slice(start, start + self.block_rows)
            slab = slice(start, start + self.slab_rows)
            dqueries, dkeys, dvalues = attend_back(
                self.queries[own],
                self.key_pad[slab],
                self.value_pad[slab],
                self.masks[index],
                self.scale,
                self.logsums[index],
                self.mixed[own],
                dmixed[own],
            )
            dquery_parts.append(dqueries)
            dkey_pad = dkey_pad.at[slab].add(dkeys)
            dvalue_pad = dvalue_pad.at[slab].add(dvalues)
        inner = slice(HALO, HALO + total_len)
        tables = (self.cos_table, self.sin_table)
        parts = [
            unrotate(jnp.concatenate(dquery_parts, axis=0), *tables),
            unrotate(dkey_pad[inner], *tables),
            dvalue_pad[inner],
        ]
        return jnp.concatenate(
            [part.reshape(total_len, self.width) for part in parts], axis=1
        ).astype(jnp.bfloat16)


def dot(left, right, left_dim, right_dim):
    return lax.dot_general(
        left,
        right,
        (((left_dim,), (right_dim,)), ((), ())),
        preferred_element_type=jnp.float32,
    )


def padded_to_lanes(values):
    return jnp.pad(values, ((0, 0), (0, -values.shape[1] % LANES)))


def high_and_low(gain):
    high = gain.astype(jnp.bfloat16)
    return [high[:, None], (gain - high.astype(jnp.float32)).astype(jnp.bfloat16)[:, None]]


def per_device(
    devices,
    seq_size,
    tokens,
    segments,
    cotangent,
    qkv_weight,
    out_weight,
    in_weight,
    down_weight,
    attn_gain,
    mlp_gain,
):
    layer_in = tokens[0]
    seg_local = segments[0]
    cot_local = cotangent[0]
    own_rows, model_width = layer_in.shape
    head_size = model_width // HEADS
    local_width = qkv_weight.shape[2]
    local_hidden = in_weight.shape[2]
    shard_rows = qkv_weight.shape[0]
    total_len = own_rows * seq_size
    paired = (
        seq_size == 2
        and total_len <= 512
        and local_width % LANES == 0
        and head_size == 2 * HEAD_HALF
    )
    swap = [(0, 1), (1, 0)]

    def rows_of_all(values):
        if paired:
            return jnp.concatenate([values, lax.ppermute(values, "seq", swap)], axis=0)
        return lax.all_gather(values, "seq", axis=0, tiled=True)

    def sum_to_owner(partial):
        if paired:
            other = lax.ppermute(partial[own_rows:].astype(jnp.bfloat16), "seq", swap)
            return partial[:own_rows] + other.astype(jnp.float32)
        return lax.psum_scatter(
            partial.astype(jnp.bfloat16), "seq", scatter_dimension=0, tiled=True
        ).astype(jnp.float32)

    def sum_over_seq(part):
        if paired:
            return part + lax.ppermute(part, "seq", swap)
        return lax.psum(part, "seq")

    first_pack = jnp.concatenate(
        [qkv_weight.reshape(shard_rows, 3 * local_width), out_weight.T], axis=1
    )
    wide = (local_hidden + 4 + LANES - 1) // LANES * LANES
    spare = jnp.zeros((shard_rows, wide - local_hidden), jnp.bfloat16)
    second_pack = jnp.concatenate(
        [in_weight[:, 0, :], spare, in_weight[:, 1, :], spare, down_weight.T]
        + high_and_low(attn_gain)
        + high_and_low(mlp_gain)
        + [spare[:, 4:]],
        axis=1,
    )
    first_full, second_full = ring_gather([first_pack, second_pack], devices)
    full_qkv = first_full[:, : 3 * local_width]
    full_out = first_full[:, 3 * local_width : 4 * local_width]
    gains_at = 2 * wide + local_hidden
    gains = second_full[:, gains_at : gains_at + 4].astype(jnp.float32)
    gain_attn = gains[:, 0] + gains[:, 1]
    gain_mlp = gains[:, 2] + gains[:, 3]
    full_in = second_full[:, : 2 * wide]
    full_down = second_full[:, 2 * wide :]

    inputs32 = layer_in.astype(jnp.float32)
    if paired:
        arrived = lax.ppermute(jnp.concatenate([layer_in, cot_local], axis=0), "seq", swap)
        all_inputs32 = jnp.concatenate([layer_in, arrived[:own_rows]], axis=0).astype(jnp.float32)
        cot_full = jnp.concatenate([cot_local, arrived[own_rows:]], axis=0)
    else:
        all_inputs32 = rows_of_all(layer_in).astype(jnp.float32)
        cot_full = rows_of_all(cot_local)
    normed_full = norm_forward(all_inputs32, gain_attn)[0].astype(jnp.bfloat16)
    unit_one, inv_one = norm_forward(inputs32, gain_attn)[1:]
    if paired:
        seg_full = rows_of_all(
            jnp.broadcast_to(seg_local.astype(jnp.float32)[:, None], (own_rows, LANES))
        )[:, 0].astype(jnp.int32)
        place = lax.axis_index("seq")
        arange = jnp.arange(own_rows, dtype=jnp.int32)
        positions = jnp.concatenate(
            [place * own_rows + arange, (1 - place) * own_rows + arange], axis=0
        )
        attention = PairedAttention(positions, seg_full, head_size, local_width)
    else:
        seg_full = rows_of_all(seg_local.astype(jnp.bfloat16)).astype(jnp.int32)
        positions = jnp.arange(total_len, dtype=jnp.int32)
        attention = BlockAttention(positions, seg_full, head_size, local_width)

    mixed = attention.forward(dot(normed_full, full_qkv, 1, 0))
    residual = inputs32 + sum_to_owner(dot(mixed, full_out, 1, 1))
    normed_two, unit_two, inv_two = norm_forward(residual, gain_mlp)
    normed_two_full = rows_of_all(normed_two.astype(jnp.bfloat16))
    expanded = dot(normed_two_full, full_in, 1, 0)
    gate_in = expanded[:, :wide]
    linear_in = expanded[:, wide:]
    activated = gelu_value(gate_in)
    middle_b = (activated * linear_in).astype(jnp.bfloat16)
    down_part = dot(middle_b, full_down, 1, 1)

    down_grad = dot(cot_full, middle_b, 0, 0).astype(jnp.bfloat16)
    dmiddle = dot(cot_full, full_down, 1, 0)
    dexpanded_b = jnp.concatenate(
        [dmiddle * linear_in * gelu_slope(gate_in), dmiddle * activated], axis=1
    ).astype(jnp.bfloat16)
    dnormed_two = sum_to_owner(dot(dexpanded_b, full_in, 1, 1))
    in_grad = dot(normed_two_full, dexpanded_b, 0, 0).astype(jnp.bfloat16)
    dres_norm, mlp_gain_part = norm_backward(dnormed_two, gain_mlp, unit_two, inv_two)
    dresidual = cot_local.astype(jnp.float32) + dres_norm
    dres_full = rows_of_all(dresidual.astype(jnp.bfloat16))
    down_part, dres_full = lax.optimization_barrier((down_part, dres_full))
    layer_out = (residual + sum_to_owner(down_part)).astype(jnp.bfloat16)
    dmixed = dot(dres_full, full_out, 1, 0).astype(jnp.bfloat16)
    out_grad = dot(dres_full, mixed, 0, 0).astype(jnp.bfloat16)
    dqkv_b = attention.backward(dmixed)
    layer_out, dqkv_b = lax.optimization_barrier((layer_out, dqkv_b))
    dnormed_one = sum_to_owner(dot(dqkv_b, full_qkv, 1, 1))
    qkv_grad = dot(normed_full, dqkv_b, 0, 0).astype(jnp.bfloat16)
    dinput_norm, attn_gain_part = norm_backward(dnormed_one, gain_attn, unit_one, inv_one)
    tokens_grad = (dresidual + dinput_norm).astype(jnp.bfloat16)
    gain_sums = sum_over_seq(jnp.stack([attn_gain_part, mlp_gain_part]))
    gain_grad = padded_to_lanes(gain_sums.T).astype(jnp.bfloat16)

    in_share, qkv_share, down_share, out_share, gain_share = ring_scatter(
        [in_grad, qkv_grad, down_grad, out_grad, gain_grad], devices
    )
    return (
        layer_out[None],
        tokens_grad[None],
        qkv_share.reshape(shard_rows, 3, local_width),
        out_share.T,
        jnp.stack([in_share[:, :local_hidden], in_share[:, wide : wide + local_hidden]], axis=1),
        down_share[:, :local_hidden].T,
        gain_share[:, 0],
        gain_share[:, 1],
    )


def solution(mesh):
    return jax.shard_map(
        functools.partial(per_device, mesh.shape["dp"], mesh.shape["seq"]),
        mesh=mesh,
        in_specs=(
            P("dp", "seq", None),
            P("dp", "seq"),
            P("dp", "seq", None),
            P("dp", None, "seq"),
            P("seq", "dp"),
            P("dp", None, "seq"),
            P("seq", "dp"),
            P("dp"),
            P("dp"),
        ),
        out_specs=(
            P("dp", "seq", None),
            P("dp", "seq", None),
            P("dp", None, "seq"),
            P("seq", "dp"),
            P("dp", None, "seq"),
            P("seq", "dp"),
            P("dp"),
            P("dp"),
        ),
        check_vma=False,
    )
```
